128 devices in a mesh: prow: 64 (over z, y, x), pcol: 2 (over core).
Axes of the slice: x: 4, y: 4, z: 4, core: 2. Of those that a mesh axis runs over, the one named last changes fastest.
Arguments:
- matrix: float32 [4, 64, 128, 32, 2, 128], P(None, 'prow', None, None, 'pcol'), may hold values from -6 to 6
- pivots: int32 [2, 128], replicated, may hold values from 0 to 32767, as said below
- upper_inverse: float32 [2, 128, 128], replicated, may hold values from -0.046875 to 0.046875
- lower_inverse: float32 [2, 128, 128], replicated, may hold values from -0.5 to 0.5
Outputs:
- factored: float32 [4, 64, 128, 32, 2, 128], P(None, 'prow', None, None, 'pcol')
The draws below stay inside these ranges and needn't reach their ends.
Inputs may be any that keep to these rules, and one draw needn't show every extreme that they name: pivots[k, i] lies between k * 128 + i and 32767.
All inputs are finite; a program needn't handle non-finite values.
Results may differ from the reference program's by a relative error of at most 0.0001.
Values sent between devices are 32-bit elements; how exact they have to be, the bound alone decides.
No kernel may reach another device: no remote copies, remote signals or barrier semaphores. Data moves between devices by JAX's collectives and lax.ppermute only.
A program may use at most 128 MiB of HBM per device.

```python
import jax
import jax.numpy as jnp
from jax import lax

NB = 128
RB_DEV = 4
CB_DEV = 32
PROWS = 64
PCOLS = 2
MROWS = 32768
NCOLS = 8192


def draw_pivots(key, part):
    offsets = jnp.arange(2, dtype=jnp.int32)[:, None] * NB + jnp.arange(NB, dtype=jnp.int32)[None, :]
    raw_values = jax.random.randint(key, (2, NB), 0, 2 ** 30, dtype=jnp.int32)
    drawn = (offsets + raw_values % (MROWS - offsets)).astype(jnp.int32)
    return drawn.at[1, NB - 1].set(MROWS - 1).astype(jnp.int32)


def shard_levels(key, shape, pieces, low, top_value):
    def one(axis_at, blocks):
        steps = jax.random.uniform(jax.random.fold_in(jax.random.fold_in(key, 6), axis_at), (blocks,), jnp.float32, low / len(pieces), top_value / len(pieces))
        return jnp.repeat(jnp.exp(steps), shape[axis_at] // blocks).reshape((-1,) + (1,) * (len(shape) - axis_at - 1))

    gain = one(*pieces[0])
    for cut in pieces[1:]:
        gain = gain * one(*cut)
    return gain


def normal_values(own_key, shape, spread, bound, split=(), kind=jnp.bfloat16):
    loudness = shard_levels(own_key, shape, split, -0.22, 0.18) if split else 1.0
    array = jax.random.normal(own_key, shape, jnp.float32) * spread * loudness
    return jnp.minimum(jnp.maximum(array, -bound), bound).astype(kind)


def setup_inputs(seed: int = 0) -> dict:
    key_of = jax.random.split(jax.random.key(seed), 5)
    return {
        "matrix": normal_values(key_of[0], (RB_DEV, PROWS, NB, CB_DEV, PCOLS, NB), 1.0, 6.0, ((1, 64), (4, 2)), jnp.float32),
        "pivots": draw_pivots(jax.random.fold_in(key_of[4], 71), 0),
        "upper_inverse": normal_values(key_of[2], (2, NB, NB), (NB * NB) ** -0.5, 0.046875, (), jnp.float32),
        "lower_inverse": normal_values(key_of[3], (2, NB, NB), NB ** -0.5, 0.5, (), jnp.float32),
    }


def build_permutation(row_pivots, step_index, row_count):
    def swap_one(position, permutation):
        target = step_index * NB + position
        chosen = row_pivots[position]
        at_target = permutation[target]
        at_chosen = permutation[chosen]
        return permutation.at[target].set(at_chosen).at[chosen].set(at_target)
    return lax.fori_loop(0, NB, swap_one, jnp.arange(row_count, dtype=jnp.int32))


def panel_step(working, step_index, row_pivots, upper_factor, lower_factor):
    permutation = build_permutation(row_pivots, step_index, MROWS)
    working = jnp.take(working, permutation, axis=0)
    below = (jnp.arange(MROWS) // NB > step_index)[:, None]
    right = (jnp.arange(NCOLS) // NB > step_index)[None, :]
    first_row = step_index * NB
    panel_part = working[:, first_row:first_row + NB]
    block_part = working[first_row:first_row + NB, :]
    lower_panel = jnp.where(below, jnp.dot(panel_part, jnp.triu(upper_factor), precision=lax.Precision.HIGHEST, preferred_element_type=jnp.float32), 0.0)
    unit_lower = jnp.tril(lower_factor, -1) + jnp.eye(NB, dtype=jnp.float32)
    upper_rows = jnp.where(right, jnp.dot(unit_lower, block_part, precision=lax.Precision.HIGHEST, preferred_element_type=jnp.float32), 0.0)
    working = working - jnp.dot(lower_panel, upper_rows, precision=lax.Precision.HIGHEST, preferred_element_type=jnp.float32)
    working = working.at[first_row:first_row + NB, :].set(jnp.where(right, upper_rows, block_part))
    working = working.at[:, first_row:first_row + NB].set(jnp.where(below, lower_panel, panel_part))
    return working


def reference(matrix, pivots, upper_inverse, lower_inverse):
    working = matrix.reshape(MROWS, NCOLS)
    for step_index in range(2):
        working = panel_step(working, step_index, pivots[step_index], upper_inverse[step_index], lower_inverse[step_index])
    return working.reshape(matrix.shape)
```

```python
import jax
import jax.numpy as jnp
from jax import lax
from jax.experimental import pallas as pl
from jax.experimental.pallas import tpu as pltpu
from jax.sharding import PartitionSpec as P

NB = 128
PICKS = 2 * NB
GROUP = 8
HBM = pl.BlockSpec(memory_space=pl.ANY)
SMEM = pl.BlockSpec(memory_space=pltpu.SMEM)
VMEM = pl.BlockSpec(memory_space=pltpu.VMEM)


def place_of(row, grid_rows):
    block = row // NB
    return block % grid_rows, block // grid_rows * NB + row % NB


def route_kernel(grid_rows, place, pivots, rows_hbm, _, slots_hbm, counts, moved_row, moved_slot, source, sems):
    me = place[0]

    def start(i, carry):
        source[i] = i
        source[pivots[i]] = pivots[i]
        return carry

    lax.fori_loop(0, PICKS, start, 0)

    def reset(i, carry):
        source[i] = i
        return carry

    lax.fori_loop(0, PICKS, reset, 0)

    def exchange(i, carry):
        chosen = pivots[i]
        at_target = source[i]
        at_chosen = source[chosen]
        source[i] = at_chosen
        source[chosen] = at_target
        return carry

    lax.fori_loop(0, PICKS, exchange, 0)

    def copy_of(slot, local):
        return pltpu.make_async_copy(rows_hbm.at[local], slots_hbm.at[slot], sems.at[slot])

    def send(i, carry):
        owner, local = place_of(source[i], grid_rows)

        @pl.when(owner == me)
        def _():
            copy_of(i, local).start()

        return carry

    lax.fori_loop(0, PICKS, send, 0)

    def send_previous(j, carry):
        @pl.when(me == j)
        def _():
            pltpu.make_async_copy(
                rows_hbm.at[pl.ds(0, NB)], slots_hbm.at[pl.ds(PICKS + j * NB, NB)], sems.at[PICKS]
            ).start()

        return carry

    lax.fori_loop(0, 2, send_previous, 0)

    def list_moved(i, count):
        chosen = pivots[i]
        owner, local = place_of(chosen, grid_rows)
        mine = jnp.logical_and(owner == me, chosen >= PICKS)

        @pl.when(mine)
        def _():
            moved_row[count] = local
            moved_slot[count] = PICKS + source[chosen]

        return count + mine.astype(jnp.int32)

    counts[0] = lax.fori_loop(0, PICKS, list_moved, 0)

    def finish(i, carry):
        owner, local = place_of(source[i], grid_rows)

        @pl.when(owner == me)
        def _():
            copy_of(i, local).wait()

        return carry

    lax.fori_loop(0, PICKS, finish, 0)

    @pl.when(me < 2)
    def _():
        pltpu.make_async_copy(
            rows_hbm.at[pl.ds(0, NB)], slots_hbm.at[pl.ds(PICKS, NB)], sems.at[PICKS]
        ).wait()


def route(place, pivots, rows, grid_rows):
    slots = jax.ShapeDtypeStruct((2 * PICKS,) + rows.shape[1:], rows.dtype)
    table = jax.ShapeDtypeStruct((PICKS,), jnp.int32)
    return pl.pallas_call(
        lambda *refs: route_kernel(grid_rows, *refs),
        out_shape=(slots, jax.ShapeDtypeStruct((1,), jnp.int32), table, table),
        in_specs=[SMEM, SMEM, HBM, HBM],
        out_specs=(HBM, SMEM, SMEM, SMEM),
        scratch_shapes=[
            pltpu.SMEM((rows.shape[0] * grid_rows,), jnp.int32),
            pltpu.SemaphoreType.DMA((PICKS + 1,)),
        ],
        input_output_aliases={3: 0},
        name="route",
    )(place, pivots, rows, jnp.zeros(slots.shape, slots.dtype))


def dot(left, right):
    return jnp.dot(left, right, precision=lax.Precision.HIGHEST, preferred_element_type=jnp.float32)


def halves(value):
    high = value.astype(jnp.bfloat16)
    return high, (value - high.astype(jnp.float32)).astype(jnp.bfloat16)


def update_kernel(
    place, counts, moved_row, moved_slot, panel, slot_panel, upper_inverse, lower_inverse,
    rows_hbm, slots_hbm, out_hbm,
    rows, picked, moved, result, own_panel, high, low, row_sems, pick_sems, moved_sems, out_sems,
):
    grid_row, grid_column = place[0], place[1]
    groups = rows.shape[0]

    def fetch(sources, target, sems, count, group):
        columns = pl.ds(group * GROUP, GROUP)
        return pltpu.make_async_copy(
            sources.at[pl.ds(0, count), columns, :], target.at[group], sems.at[group]
        )

    def fetch_moved(i):
        return pltpu.make_async_copy(slots_hbm.at[moved_slot[i]], moved.at[i], moved_sems.at[i])

    for group in range(groups):
        fetch(slots_hbm, picked, pick_sems, PICKS, group).start()
        fetch(rows_hbm, rows, row_sems, rows.shape[1], group).start()

    def start_moved(i, carry):
        fetch_moved(i).start()
        return carry

    lax.fori_loop(0, counts[0], start_moved, 0)

    own_panel[...] = panel[...]

    def patch_panel(i, carry):
        for side in range(2):
            own_panel[side, pl.ds(moved_row[i], 1), :] = slot_panel[side, pl.ds(moved_slot[i], 1), :]
        return carry

    lax.fori_loop(0, counts[0], patch_panel, 0)

    row_at = lax.broadcasted_iota(jnp.int32, (NB, NB), 0)
    column_at = lax.broadcasted_iota(jnp.int32, (NB, NB), 1)
    upper = [jnp.where(row_at <= column_at, upper_inverse[k], 0.0) for k in range(2)]
    lower = [
        jnp.where(row_at > column_at, lower_inverse[k], jnp.where(row_at == column_at, 1.0, 0.0))
        for k in range(2)
    ]
    block_lower = dot(slot_panel[0, NB:PICKS, :], upper[0])
    block_upper = dot(lower[0], slot_panel[1, :NB, :])
    block_second = slot_panel[1, NB:PICKS, :] - dot(block_lower, block_upper)
    mixed = -dot(lower[1], dot(block_lower, lower[0]))
    lower_first = dot(own_panel[0], upper[0])
    lower_second = dot(own_panel[1] - dot(lower_first, block_upper), upper[1])
    weight_first = dot(lower_first, lower[0]) + dot(lower_second, mixed)
    weight_second = dot(lower_second, lower[1])
    first_home, second_home = grid_row == 0, grid_row == 1
    is_home = grid_row < 2

    def at_home(first, second, other):
        top = jnp.where(first_home, first, jnp.where(second_home, second, other[:NB]))
        return jnp.concatenate([top, other[NB:]], axis=0)

    weight = jnp.concatenate(
        [
            at_home(-lower[0], -mixed, weight_first),
            at_home(jnp.zeros_like(lower[1]), -lower[1], weight_second),
        ],
        axis=1,
    )
    high[...], low[...] = halves(weight)
    head = jnp.where(
        grid_column == 0,
        at_home(slot_panel[0, :NB, :], block_lower, lower_first),
        at_home(block_upper, block_second, lower_second),
    )

    def wait_moved(i, carry):
        fetch_moved(i).wait()
        return carry

    lax.fori_loop(0, counts[0], wait_moved, 0)

    def write(group, slot):
        return pltpu.make_async_copy(
            result.at[slot], out_hbm.at[:, pl.ds(group * GROUP, GROUP), :], out_sems.at[slot]
        )

    for group in range(groups):
        slot = group % 2
        fetch(rows_hbm, rows, row_sems, rows.shape[1], group).wait()
        fetch(slots_hbm, picked, pick_sems, PICKS, group).wait()

        def patch(i, carry):
            rows[group, moved_row[i], :, :] = moved[i, pl.ds(group * GROUP, GROUP), :]
            return carry

        lax.fori_loop(0, counts[0], patch, 0)
        if group >= 2:
            write(group - 2, slot).wait()
        for pair in range(GROUP // 2):
            columns = [2 * pair, 2 * pair + 1]
            right = jnp.concatenate([picked[group, :, c, :] for c in columns], axis=1)
            right_high, right_low = halves(right)
            product = jnp.dot(high[...], right_high, preferred_element_type=jnp.float32)
            product += jnp.dot(high[...], right_low, preferred_element_type=jnp.float32)
            product += jnp.dot(low[...], right_high, preferred_element_type=jnp.float32)
            for n, c in enumerate(columns):
                own = rows[group, :, c, :]
                top = jnp.where(is_home, 0.0, own[:NB])
                own = jnp.concatenate([top, own[NB:]], axis=0)
                value = own - product[:, n * NB : (n + 1) * NB]
                if group == 0 and c == 0:
                    value = head
                result[slot, :, c, :] = value
        write(group, slot).start()
    for group in range(max(0, groups - 2), groups):
        write(group, group % 2).wait()


def update(place, counts, moved_row, moved_slot, panel, slot_panel, upper_inverse, lower_inverse, rows, slots):
    local_rows, blocks, _ = rows.shape
    groups = blocks // GROUP
    return pl.pallas_call(
        update_kernel,
        out_shape=jax.ShapeDtypeStruct(rows.shape, rows.dtype),
        in_specs=[SMEM] * 4 + [VMEM] * 4 + [HBM] * 2,
        out_specs=HBM,
        scratch_shapes=[
            pltpu.VMEM((groups, local_rows, GROUP, NB), jnp.float32),
            pltpu.VMEM((groups, PICKS, GROUP, NB), jnp.float32),
            pltpu.VMEM((PICKS, blocks, NB), jnp.float32),
            pltpu.VMEM((2, local_rows, GROUP, NB), jnp.float32),
            pltpu.VMEM((2, local_rows, NB), jnp.float32),
            pltpu.VMEM((local_rows, PICKS), jnp.bfloat16),
            pltpu.VMEM((local_rows, PICKS), jnp.bfloat16),
            pltpu.SemaphoreType.DMA((groups,)),
            pltpu.SemaphoreType.DMA((groups,)),
            pltpu.SemaphoreType.DMA((PICKS,)),
            pltpu.SemaphoreType.DMA((2,)),
        ],
        compiler_params=pltpu.CompilerParams(vmem_limit_bytes=48 << 20),
        name="update",
    )(place, counts, moved_row, moved_slot, panel, slot_panel, upper_inverse, lower_inverse, rows, slots)


def local(matrix, pivots, upper_inverse, lower_inverse):
    grid_rows = lax.axis_size("prow")
    rows = matrix.reshape(matrix.shape[0] * NB, matrix.shape[3], NB)
    place = jnp.stack([lax.axis_index("prow"), lax.axis_index("pcol")]).astype(jnp.int32)
    panel = lax.all_gather(rows[:, 0, :], "pcol", axis=0)
    slots, counts, moved_row, moved_slot = route(place, pivots.reshape(-1), rows, grid_rows)
    slots = lax.psum(slots, "prow")
    slot_panel = lax.all_gather(slots[:, 0, :], "pcol", axis=0)
    out = update(
        place, counts, moved_row, moved_slot, panel, slot_panel, upper_inverse, lower_inverse, rows, slots
    )
    return out.reshape(matrix.shape)


def solution(mesh):
    return jax.shard_map(
        local,
        mesh=mesh,
        in_specs=(P(None, "prow", None, None, "pcol", None), P(), P(), P()),
        out_specs=P(None, "prow", None, None, "pcol", None),
        check_vma=False,
    )
```

```python
import jax
import jax.numpy as jnp
from jax import lax
from jax.experimental import pallas as pl
from jax.experimental.pallas import tpu as pltpu
from jax.sharding import PartitionSpec as P

NB = 128
PICKS = 2 * NB
SIDE = 4
PLANE = SIDE * SIDE
SHARE = PICKS // PLANE
GROUP = 8
OFFSETS = (0, -1, 1, 2)
HBM = pl.BlockSpec(memory_space=pl.ANY)
SMEM = pl.BlockSpec(memory_space=pltpu.SMEM)
VMEM = pl.BlockSpec(memory_space=pltpu.VMEM)


def chip(z, y, x):
    return (z % SIDE * SIDE + y % SIDE) * SIDE + x % SIDE


def moves(dz, dy, dx):
    span = range(SIDE)
    return [(chip(z, y, x), chip(z + dz, y + dy, x + dx)) for z in span for y in span for x in span]


def owner_of(row):
    return (row >> 7) & (SIDE * PLANE - 1)


def local_of(row):
    return ((row >> 13) << 7) | (row & (NB - 1))


def each(count, body, unroll=8):
    def step(i, carry):
        body(i)
        return carry

    lax.fori_loop(0, count, step, 0, unroll=unroll)


def route_kernel(
    place, pivots, rows_hbm,
    send_hbm, pick_row, hub_source, stats, moved_row, moved_first, moved_second, order_first, order_second,
    source, rank_of, begin, sems,
):
    me = place[0]
    plane_at = me % PLANE
    my_y, my_x = plane_at // SIDE, plane_at % SIDE

    def start(i):
        chosen = pivots[i]
        source[chosen] = chosen

    each(PICKS, start)

    def reset(i):
        source[i] = i

    each(PICKS, reset)

    def exchange(i):
        chosen = pivots[i]
        at_target = source[i]
        at_chosen = source[chosen]
        source[i] = at_chosen
        source[chosen] = at_target

    each(PICKS, exchange, 4)

    def clear(o):
        begin[o] = 0

    each(SIDE * PLANE, clear)

    def count(i):
        owner = owner_of(source[i])
        before = begin[owner]
        rank_of[i] = before
        begin[owner] = before + 1

    each(PICKS, count, 4)

    def prefix(o, carry):
        total, most = carry
        held = begin[o]
        begin[o] = total
        return total + held, jnp.maximum(most, held)

    _, most = lax.fori_loop(0, SIDE * PLANE, prefix, (0, 0), unroll=4)
    stats[0] = most
    mine = begin[me]

    def deal(i):
        row = source[i]
        rank = begin[owner_of(row)] + rank_of[i]
        rank_of[i] = rank
        pick_row[rank] = row
        order_first[rank] = i

    each(PICKS, deal, 4)
    last = jnp.where(me == SIDE * PLANE - 1, PICKS, begin[jnp.minimum(me + 1, SIDE * PLANE - 1)])
    sent = jnp.minimum(last - mine, SHARE)

    def copy_of(n, z):
        rank = mine + n
        return pltpu.make_async_copy(
            rows_hbm.at[local_of(pick_row[rank])],
            send_hbm.at[z * PLANE + rank % PLANE],
            sems.at[n * SIDE + z],
        )

    def send(n, carry):
        for z in range(SIDE):
            copy_of(n, z).start()
        return carry

    lax.fori_loop(0, sent, send, 0)

    def hub(t):
        hub_source[t] = owner_of(pick_row[t * PLANE + plane_at])

    each(SHARE, hub)

    def list_moved(i, found):
        chosen = pivots[i]
        is_mine = jnp.logical_and(owner_of(chosen) == me, chosen >= PICKS)

        @pl.when(is_mine)
        def _():
            previous = source[chosen]
            kept = previous % NB
            x = previous // NB + 2 * (kept % 32 // SHARE)
            y = kept // 32
            dx, dy = (x - my_x) % SIDE, (y - my_y) % SIDE
            at_x = jnp.where(dx == 3, 1, jnp.where(dx == 0, 0, dx + 1))
            at_y = jnp.where(dy == 3, 1, jnp.where(dy == 0, 0, dy + 1))
            moved_row[found] = local_of(chosen)
            moved_first[found] = (at_y * SIDE + at_x) * 2 * SHARE + SHARE + kept % SHARE
            moved_second[found] = (at_x * SIDE + at_y) * 2 * SHARE + SHARE + kept % SHARE

        return found + is_mine.astype(jnp.int32)

    stats[1] = lax.fori_loop(0, PICKS, list_moved, 0, unroll=4)

    def tag(i):
        rank_of[order_first[i]] = i

    def keep(i):
        order_second[i] = order_first[i]

    each(PICKS, keep)

    def name_first(t):
        for a, dy in enumerate(OFFSETS):
            for b, dx in enumerate(OFFSETS):
                column = (my_y + dy) % SIDE * SIDE + (my_x + dx) % SIDE
                order_first[(a * SIDE + b) * SHARE + t] = order_second[t * PLANE + column]

    each(SHARE, name_first, 1)

    def finish(n, carry):
        for z in range(SIDE):
            copy_of(n, z).wait()
        return carry

    lax.fori_loop(0, sent, finish, 0)


def route(place, pivots, rows):
    table = jax.ShapeDtypeStruct((PICKS,), jnp.int32)
    small = jax.ShapeDtypeStruct((SHARE,), jnp.int32)
    chips = SIDE * PLANE
    return pl.pallas_call(
        route_kernel,
        out_shape=(
            jax.ShapeDtypeStruct((chips,) + rows.shape[1:], rows.dtype), table, small, small,
            table, table, table, table, table,
        ),
        in_specs=[SMEM, SMEM, HBM],
        out_specs=(HBM,) + (SMEM,) * 8,
        scratch_shapes=[
            pltpu.SMEM((rows.shape[0] * chips,), jnp.int32),
            pltpu.SMEM((PICKS,), jnp.int32),
            pltpu.SMEM((chips,), jnp.int32),
            pltpu.SemaphoreType.DMA((SHARE * SIDE,)),
        ],
        cost_estimate=pl.CostEstimate(flops=0, transcendentals=0, bytes_accessed=30_000_000),
        name="route",
    )(place, pivots, rows)


def round_kernel(at, place, pick_row, rows_hbm, send_hbm, sems):
    me = place[0]

    def copy_of(h, z):
        row = pick_row[at[0] * PLANE + h]
        copy = pltpu.make_async_copy(
            rows_hbm.at[local_of(row)], send_hbm.at[z * PLANE + h], sems.at[h * SIDE + z]
        )
        return owner_of(row) == me, copy

    def go(h):
        for z in range(SIDE):
            held, copy = copy_of(h, z)
            pl.when(held)(copy.start)

    each(PLANE, go, 1)

    def finish(h):
        for z in range(SIDE):
            held, copy = copy_of(h, z)
            pl.when(held)(copy.wait)

    each(PLANE, finish, 1)


def send_round(at, place, pick_row, rows):
    return pl.pallas_call(
        round_kernel,
        out_shape=jax.ShapeDtypeStruct((SIDE * PLANE,) + rows.shape[1:], rows.dtype),
        in_specs=[SMEM, SMEM, SMEM, HBM],
        out_specs=HBM,
        scratch_shapes=[pltpu.SemaphoreType.DMA((PLANE * SIDE,))],
        name="send_round",
    )(at, place, pick_row, rows)


def swap_all(rows):
    return lax.all_to_all(rows, "prow", 0, 0, tiled=True)


def crowded(place, pick_row, hub_source, rows, received):
    def step(t, held):
        sent = send_round(jnp.full((1,), t, jnp.int32), place, pick_row, rows)
        row = lax.dynamic_slice_in_dim(swap_all(sent), hub_source[t], 1, axis=0)
        return lax.dynamic_update_slice_in_dim(held, row, t, axis=0)

    held = lax.fori_loop(0, SHARE, step, jnp.zeros_like(received))
    return held, jnp.arange(SHARE, dtype=jnp.int32)


def pack_kernel(place, index, received, own, first, second, third, left, right, buffer, sems, out_sems):
    z = place[0] // PLANE

    def pick(t):
        return pltpu.make_async_copy(received.at[index[t]], buffer.at[t], sems.at[t])

    each(SHARE, lambda t: pick(t).start())
    for level, held in enumerate((own, first, second, third)):

        @pl.when(z == level)
        def _():
            pltpu.make_async_copy(held, buffer.at[pl.ds(SHARE, SHARE)], sems.at[SHARE]).start()

    each(SHARE, lambda t: pick(t).wait())
    pltpu.make_async_copy(own, buffer.at[pl.ds(SHARE, SHARE)], sems.at[SHARE]).wait()
    half = left.shape[1]
    outs = [
        pltpu.make_async_copy(buffer.at[:, pl.ds(n * half, half), :], out, out_sems.at[n])
        for n, out in enumerate((left, right))
    ]
    for out in outs:
        out.start()
    for out in outs:
        out.wait()


def pack(place, index, received, previous):
    blocks, width = received.shape[1:]
    out = jax.ShapeDtypeStruct((2 * SHARE, blocks // 2, width), received.dtype)
    return pl.pallas_call(
        pack_kernel,
        out_shape=(out, out),
        in_specs=[SMEM, SMEM] + [HBM] * 5,
        out_specs=(HBM, HBM),
        scratch_shapes=[
            pltpu.VMEM((2 * SHARE, blocks, width), received.dtype),
            pltpu.SemaphoreType.DMA((SHARE + 1,)),
            pltpu.SemaphoreType.DMA((2,)),
        ],
        name="pack",
    )(place, index, received, *previous)


def permute(value, pairs):
    return lax.ppermute(value, "prow", pairs)


def spread_previous(block, me):
    y, x = me // SIDE % SIDE, me % SIDE
    quarter = 2 * SHARE
    homes = (0, 1)
    parts = [
        permute(block[quarter * n : quarter * (n + 1)], [(h, chip(0, n, h)) for h in homes])
        for n in range(1, SIDE)
    ]
    held = block[:quarter]
    for n, part in enumerate(parts):
        held = jnp.where(y == n + 1, part, held)
    across = permute(
        held[SHARE:], [(chip(0, n, h), chip(0, n, h + 2)) for n in range(SIDE) for h in homes]
    )
    own = jnp.where(x < 2, held[:SHARE], across)
    plane = [(n, n % PLANE) for n in range(PLANE)]
    return [own] + [permute(own, [(n, z * PLANE + n) for n, _ in plane]) for z in range(1, SIDE)]


def along(axis, offset):
    return moves(0, offset, 0) if axis == "y" else moves(0, 0, offset)


def gather_line(value, axis):
    pieces = [permute(value, along(axis, -offset)) for offset in OFFSETS[1:]]
    return jnp.concatenate([value] + pieces, axis=0)


def gather_plane(value, axis, other):
    line = gather_line(value, axis)
    before = permute(line, along(other, 1))
    after = permute(line, along(other, -1))
    half = line.shape[0] // 2
    far_low = permute(before[:half], along(other, 1))
    far_high = permute(after[half:], along(other, -1))
    return [line, before, after, far_low, far_high]


def dot(left, right):
    return jnp.dot(left, right, precision=lax.Precision.HIGHEST, preferred_element_type=jnp.float32)


def single(left, right):
    return jnp.dot(left, right, preferred_element_type=jnp.float32)


def halves(value):
    high = value.astype(jnp.bfloat16)
    return high, (value - high.astype(jnp.float32)).astype(jnp.bfloat16)


def update_kernel(*refs):
    place, stats, moved_row, moved_first, moved_second = refs[:5]
    panel, slot_panel, order_first, order_second, upper_inverse, lower_inverse = refs[5:11]
    rows_hbm, pieces, out_hbm = refs[11], (refs[12:17], refs[17:22]), refs[22]
    rows, plane, result, own_panel, weights, row_sems, piece_sems, out_sems = refs[23:]
    grid_row, grid_column = place[0], place[1]
    groups, local_rows = rows.shape[:2]
    per_half = groups // 2

    def fetch_rows(group):
        columns = pl.ds(group * GROUP, GROUP)
        return pltpu.make_async_copy(rows_hbm.at[:, columns, :], rows.at[group], row_sems.at[group])

    def fetch_piece(side, n):
        piece = pieces[side][n]
        begin = (0, 8 * SHARE, 16 * SHARE, 24 * SHARE, 28 * SHARE)[n]
        target = plane.at[side, pl.ds(begin, piece.shape[0])]
        return pltpu.make_async_copy(piece, target, piece_sems.at[side, n])

    for side in range(2):
        for n in range(5):
            fetch_piece(side, n).start()
        for group in range(side * per_half, (side + 1) * per_half):
            fetch_rows(group).start()

    own_panel[...] = panel[...]

    def patch_panel(i, carry):
        for side in range(2):
            own_panel[side, pl.ds(moved_row[i], 1), :] = slot_panel[side, pl.ds(moved_first[i], 1), :]
        return carry

    lax.fori_loop(0, stats[1], patch_panel, 0)

    def one_hot(order):
        return lax.broadcasted_iota(jnp.int32, (PICKS, PICKS), 0) == order[...]

    place_first = one_hot(order_first)
    row_at = lax.broadcasted_iota(jnp.int32, (NB, NB), 0)
    column_at = lax.broadcasted_iota(jnp.int32, (NB, NB), 1)
    upper = [jnp.where(row_at <= column_at, upper_inverse[k], 0.0) for k in range(2)]
    lower = [
        jnp.where(row_at > column_at, lower_inverse[k], jnp.where(row_at == column_at, 1.0, 0.0))
        for k in range(2)
    ]
    dealt = [
        jnp.concatenate([slot_panel[k, 2 * SHARE * n : 2 * SHARE * n + SHARE, :] for n in range(PLANE)], axis=0)
        for k in range(2)
    ]
    picked = dot(place_first.astype(jnp.float32), jnp.concatenate(dealt, axis=1))
    block_lower = dot(picked[NB:, :NB], upper[0])
    block_upper = dot(lower[0], picked[:NB, NB:])
    block_second = picked[NB:, NB:] - dot(block_lower, block_upper)
    mixed = -dot(lower[1], dot(block_lower, lower[0]))
    lower_first = dot(own_panel[0], upper[0])
    lower_second = dot(own_panel[1] - dot(lower_first, block_upper), upper[1])
    weight_first = dot(lower_first, lower[0]) + dot(lower_second, mixed)
    weight_second = dot(lower_second, lower[1])
    first_home, second_home = grid_row == 0, grid_row == 1
    is_home = grid_row < 2

    def at_home(first, second, other):
        top = jnp.where(first_home, first, jnp.where(second_home, second, other[:NB]))
        return jnp.concatenate([top, other[NB:]], axis=0)

    weight = jnp.concatenate(
        [
            at_home(-lower[0], -mixed, weight_first),
            at_home(jnp.zeros_like(lower[1]), -lower[1], weight_second),
        ],
        axis=1,
    )
    high, low = halves(weight)
    for side, hot in enumerate((place_first, one_hot(order_second))):
        hot = hot.astype(jnp.bfloat16)
        weights[2 * side] = single(high, hot).astype(jnp.bfloat16)
        weights[2 * side + 1] = single(low, hot).astype(jnp.bfloat16)
    head = jnp.where(
        grid_column == 0,
        at_home(picked[:NB, :NB], block_lower, lower_first),
        at_home(block_upper, block_second, lower_second),
    )

    def write(group, slot):
        return pltpu.make_async_copy(
            result.at[slot], out_hbm.at[:, pl.ds(group * GROUP, GROUP), :], out_sems.at[slot]
        )

    for group in range(groups):
        slot, side = group % 2, group // per_half
        begin = group % per_half * GROUP
        if group % per_half == 0:
            for n in range(5):
                fetch_piece(side, n).wait()
        fetch_rows(group).wait()
        moved = (moved_first, moved_second)[side]

        def patch(i, carry):
            rows[group, moved_row[i], :, :] = plane[side, moved[i], begin : begin + GROUP, :]
            return carry

        lax.fori_loop(0, stats[1], patch, 0)
        if group >= 2:
            write(group - 2, slot).wait()
        for pair in range(GROUP // 2):
            columns = [2 * pair, 2 * pair + 1]
            right = [
                jnp.concatenate(
                    [plane[side, 2 * SHARE * n : 2 * SHARE * n + SHARE, begin + c, :] for n in range(PLANE)],
                    axis=0,
                )
                for c in columns
            ]
            right_high, right_low = halves(jnp.concatenate(right, axis=1))
            product = single(weights[2 * side], right_high)
            product += single(weights[2 * side], right_low)
            product += single(weights[2 * side + 1], right_high)
            for n, c in enumerate(columns):
                own = rows[group, :, c, :]
                top = jnp.where(is_home, 0.0, own[:NB])
                own = jnp.concatenate([top, own[NB:]], axis=0)
                value = own - product[:, n * NB : (n + 1) * NB]
                if group == 0 and c == 0:
                    value = head
                result[slot, :, c, :] = value
        write(group, slot).start()
    for group in range(max(0, groups - 2), groups):
        write(group, group % 2).wait()


def update(tables, panel, slot_panel, orders, upper_inverse, lower_inverse, rows, pieces):
    local_rows, blocks, _ = rows.shape
    groups = blocks // GROUP
    orders = [order.reshape(1, PICKS) for order in orders]
    return pl.pallas_call(
        update_kernel,
        out_shape=jax.ShapeDtypeStruct(rows.shape, rows.dtype),
        in_specs=[SMEM] * 5 + [VMEM] * 6 + [HBM] * 11,
        out_specs=HBM,
        scratch_shapes=[
            pltpu.VMEM((groups, local_rows, GROUP, NB), jnp.float32),
            pltpu.VMEM((2, 2 * PICKS, blocks // 2, NB), jnp.float32),
            pltpu.VMEM((2, local_rows, GROUP, NB), jnp.float32),
            pltpu.VMEM((2, local_rows, NB), jnp.float32),
            pltpu.VMEM((4, local_rows, PICKS), jnp.bfloat16),
            pltpu.SemaphoreType.DMA((groups,)),
            pltpu.SemaphoreType.DMA((2, 5)),
            pltpu.SemaphoreType.DMA((2,)),
        ],
        compiler_params=pltpu.CompilerParams(vmem_limit_bytes=48 << 20),
        cost_estimate=pl.CostEstimate(flops=3_300_000_000, transcendentals=0, bytes_accessed=26_000_000),
        name="update",
    )(*tables, panel, slot_panel, *orders, upper_inverse, lower_inverse, rows, *pieces[0], *pieces[1])


def local(matrix, pivots, upper_inverse, lower_inverse):
    me = lax.axis_index("prow")
    rows = matrix.reshape(matrix.shape[0] * NB, matrix.shape[3], NB)
    place = jnp.stack([me, lax.axis_index("pcol")]).astype(jnp.int32)
    previous = spread_previous(rows[:NB], me)
    panel = lax.all_gather(rows[:, 0, :], "pcol", axis=0)
    sent, pick_row, hub_source, stats, moved_row, moved_first, moved_second, order_first, order = route(
        place, pivots.reshape(-1), rows
    )
    received = swap_all(sent)
    received, index = lax.cond(
        stats[0] <= SHARE,
        lambda: (received, hub_source),
        lambda: crowded(place, pick_row, hub_source, rows, received),
    )
    left, right = pack(place, index, received, previous)
    pieces = gather_plane(left, "x", "y"), gather_plane(right, "y", "x")
    order_second = order_first.reshape(SIDE, SIDE, SHARE).swapaxes(0, 1)
    heads = jnp.concatenate([piece[:, 0, :] for piece in pieces[0]], axis=0)
    slot_panel = lax.all_gather(heads, "pcol", axis=0)
    out = update(
        (place, stats, moved_row, moved_first, moved_second),
        panel, slot_panel, (order_first, order_second), upper_inverse, lower_inverse, rows, pieces,
    )
    return out.reshape(matrix.shape)


def solution(mesh):
    return jax.shard_map(
        local,
        mesh=mesh,
        in_specs=(P(None, "prow", None, None, "pcol", None), P(), P(), P()),
        out_specs=P(None, "prow", None, None, "pcol", None),
        check_vma=False,
    )
```

```python
import jax
import jax.numpy as jnp
from jax import lax
from jax.experimental import pallas as pl
from jax.experimental.pallas import tpu as pltpu
from jax.sharding import PartitionSpec as P

NB = 128
PICKS = 2 * NB
SIDE = 4
PLANE = SIDE * SIDE
SHARE = PICKS // PLANE
QUARTER = NB // SIDE
GROUP = 8
OFFSETS = (0, -1, 1, 2)
HBM = pl.BlockSpec(memory_space=pl.ANY)
SMEM = pl.BlockSpec(memory_space=pltpu.SMEM)
VMEM = pl.BlockSpec(memory_space=pltpu.VMEM)
SMALL = pltpu.CompilerParams(vmem_limit_bytes=4 << 20)


def chip(z, y, x):
    return (z % SIDE * SIDE + y % SIDE) * SIDE + x % SIDE


def moves(dz, dy, dx):
    span = range(SIDE)
    return [(chip(z, y, x), chip(z + dz, y + dy, x + dx)) for z in span for y in span for x in span]


def owner_of(row):
    return (row >> 7) & (SIDE * PLANE - 1)


def local_of(row):
    return ((row >> 13) << 7) | (row & (NB - 1))


def each(count, body, unroll=8):
    def step(i, carry):
        body(i)
        return carry

    lax.fori_loop(0, count, step, 0, unroll=unroll)


def exchange_kernel(pivots, picked, kept, source):
    def start(i):
        chosen = pivots[i]
        source[chosen] = chosen
        source[i] = i

    each(PICKS, start)

    def exchange(i):
        chosen = pivots[i]
        at_target = source[i]
        at_chosen = source[chosen]
        source[i] = at_chosen
        source[chosen] = at_target

    each(PICKS, exchange)

    def keep(i):
        picked[i] = source[i]
        kept[i] = source[pivots[i]]

    each(PICKS, keep)


def exchange(pivots, row_count):
    table = jax.ShapeDtypeStruct((PICKS,), jnp.int32)
    return pl.pallas_call(
        exchange_kernel,
        out_shape=(table, table),
        in_specs=[SMEM],
        out_specs=(SMEM, SMEM),
        scratch_shapes=[pltpu.SMEM((row_count,), jnp.int32)],
        cost_estimate=pl.CostEstimate(flops=0, transcendentals=0, bytes_accessed=60_000_000),
        compiler_params=SMALL,
        name="exchange",
    )(pivots)


def ranks_of(picked):
    owner = owner_of(picked)
    earlier = owner[None, :] < owner[:, None]
    same = owner[None, :] == owner[:, None]
    index = jnp.arange(PICKS)
    ahead = jnp.logical_or(earlier, jnp.logical_and(same, index[None, :] < index[:, None]))
    rank = jnp.sum(ahead.astype(jnp.int32), axis=1)
    return rank, jnp.max(jnp.sum(same.astype(jnp.int32), axis=1))


def deal_kernel(
    place, picked, rank, rows_hbm, send_hbm, pick_row, hub_source, own, held, held_sems, sems
):
    me = place[0]

    def note(i, count):
        row = picked[i]
        pick_row[rank[i]] = row
        own[count] = i
        return count + (owner_of(row) == me).astype(jnp.int32)

    count = jnp.minimum(lax.fori_loop(0, PICKS, note, 0, unroll=16), SHARE)

    def fetch(n):
        return pltpu.make_async_copy(rows_hbm.at[local_of(picked[own[n]])], held.at[n], held_sems.at[n])

    def copy_of(n, z):
        column = rank[own[n]] % PLANE
        return pltpu.make_async_copy(held.at[n], send_hbm.at[z * PLANE + column], sems.at[n * SIDE + z])

    def loop(body):
        def step(n, carry):
            body(n)
            return carry

        lax.fori_loop(0, count, step, 0)

    def send(n):
        fetch(n).wait()
        for z in range(SIDE):
            copy_of(n, z).start()

    def finish(n):
        for z in range(SIDE):
            copy_of(n, z).wait()

    def hub(t):
        hub_source[t] = owner_of(pick_row[t * PLANE + me % PLANE])

    loop(lambda n: fetch(n).start())
    each(SHARE, hub, 16)
    loop(send)
    loop(finish)


def deal(place, picked, rank, rows):
    chips = SIDE * PLANE
    return pl.pallas_call(
        deal_kernel,
        out_shape=(
            jax.ShapeDtypeStruct((chips,) + rows.shape[1:], rows.dtype),
            jax.ShapeDtypeStruct((PICKS,), jnp.int32),
            jax.ShapeDtypeStruct((SHARE,), jnp.int32),
        ),
        in_specs=[SMEM, SMEM, SMEM, HBM],
        out_specs=(HBM, SMEM, SMEM),
        scratch_shapes=[
            pltpu.SMEM((PICKS + 1,), jnp.int32),
            pltpu.VMEM((SHARE,) + rows.shape[1:], rows.dtype),
            pltpu.SemaphoreType.DMA((SHARE,)),
            pltpu.SemaphoreType.DMA((SHARE * SIDE,)),
        ],
        cost_estimate=pl.CostEstimate(flops=0, transcendentals=0, bytes_accessed=30_000_000),
        compiler_params=SMALL,
        name="deal",
    )(place, picked, rank, rows)


def table_kernel(place, pivots, kept, rank, moved, orders, order):
    me = place[0]
    my_y, my_x = me // SIDE % SIDE, me % SIDE

    def invert(i):
        order[rank[i]] = i

    each(PICKS, invert, 16)

    def at_offset(there, here):
        apart = (there - here) % SIDE
        return jnp.where(apart == 3, 1, jnp.where(apart == 0, 0, apart + 1))

    def list_moved(i, count):
        chosen = pivots[i]
        moved[count] = i
        is_mine = jnp.logical_and(owner_of(chosen) == me, chosen >= PICKS)
        return count + is_mine.astype(jnp.int32)

    count = lax.fori_loop(0, PICKS, list_moved, 0, unroll=16)
    moved[4 * PICKS] = count

    def name_moved(n, carry):
        i = moved[n]
        home, held = kept[i] // NB, kept[i] % NB
        x, y, t = home + 2 * (held % QUARTER // SHARE), held // QUARTER, held % SHARE
        at_x, at_y = at_offset(x, my_x), at_offset(y, my_y)
        moved[n] = local_of(pivots[i])
        moved[PICKS + n] = (at_y * SIDE + at_x) * SHARE + t
        moved[2 * PICKS + n] = (at_x * SIDE + at_y) * SHARE + t
        moved[3 * PICKS + n] = (y * SIDE + x) * 2 * SHARE + SHARE + t
        return carry

    lax.fori_loop(0, count, name_moved, 0)

    for a, dy in enumerate(OFFSETS):
        for b, dx in enumerate(OFFSETS):
            column = (my_y + dy) % SIDE * SIDE + (my_x + dx) % SIDE
            for t in range(SHARE):
                pick = order[t * PLANE + column]
                orders[(a * SIDE + b) * SHARE + t] = pick
                orders[PICKS + (b * SIDE + a) * SHARE + t] = pick
                orders[2 * PICKS + column * SHARE + t] = pick


def tables(place, pivots, kept, rank):
    return pl.pallas_call(
        table_kernel,
        out_shape=[jax.ShapeDtypeStruct((n,), jnp.int32) for n in (4 * PICKS + 1, 3 * PICKS)],
        in_specs=[SMEM] * 4,
        out_specs=[SMEM] * 2,
        scratch_shapes=[pltpu.SMEM((PICKS,), jnp.int32)],
        cost_estimate=pl.CostEstimate(flops=0, transcendentals=0, bytes_accessed=20_000_000),
        compiler_params=SMALL,
        name="tables",
    )(place, pivots, kept, rank)


def round_kernel(at, place, pick_row, rows_hbm, send_hbm, sems):
    me = place[0]

    def copy_of(h, z):
        row = pick_row[at[0] * PLANE + h]
        copy = pltpu.make_async_copy(
            rows_hbm.at[local_of(row)], send_hbm.at[z * PLANE + h], sems.at[h * SIDE + z]
        )
        return owner_of(row) == me, copy

    def go(h):
        for z in range(SIDE):
            held, copy = copy_of(h, z)
            pl.when(held)(copy.start)

    each(PLANE, go, 1)

    def finish(h):
        for z in range(SIDE):
            held, copy = copy_of(h, z)
            pl.when(held)(copy.wait)

    each(PLANE, finish, 1)


def send_round(at, place, pick_row, rows):
    return pl.pallas_call(
        round_kernel,
        out_shape=jax.ShapeDtypeStruct((SIDE * PLANE,) + rows.shape[1:], rows.dtype),
        in_specs=[SMEM, SMEM, SMEM, HBM],
        out_specs=HBM,
        scratch_shapes=[pltpu.SemaphoreType.DMA((PLANE * SIDE,))],
        compiler_params=SMALL,
        name="send_round",
    )(at, place, pick_row, rows)


def swap_all(rows):
    return lax.all_to_all(rows, "prow", 0, 0, tiled=True)


def crowded(place, pick_row, hub_source, rows, received):
    def step(t, held):
        sent = send_round(jnp.full((1,), t, jnp.int32), place, pick_row, rows)
        row = lax.dynamic_slice_in_dim(swap_all(sent), hub_source[t], 1, axis=0)
        return lax.dynamic_update_slice_in_dim(held, row, t, axis=0)

    held = lax.fori_loop(0, SHARE, step, jnp.zeros_like(received))
    return held, jnp.arange(SHARE, dtype=jnp.int32)


def pack_kernel(place, index, received, *refs):
    copies, left, right, heads, buffer, edge, sems, out_sems = refs[:SIDE], *refs[SIDE:]
    z = place[0] // PLANE

    def pick(t):
        return pltpu.make_async_copy(received.at[index[t]], buffer.at[t], sems.at[t])

    def previous(held):
        return pltpu.make_async_copy(held, buffer.at[pl.ds(SHARE, SHARE)], sems.at[SHARE])

    each(SHARE, lambda t: pick(t).start())
    for level, held in enumerate(copies):
        pl.when(z == level)(lambda held=held: previous(held).start())
    each(SHARE, lambda t: pick(t).wait())
    previous(copies[0]).wait()
    edge[...] = buffer[:, 0, :]
    half = left.shape[1]
    outs = [
        pltpu.make_async_copy(buffer.at[:, pl.ds(n * half, half), :], out, out_sems.at[n])
        for n, out in enumerate((left, right))
    ]
    outs += [
        pltpu.make_async_copy(edge, heads.at[pl.ds(n * 2 * SHARE, 2 * SHARE)], out_sems.at[2 + n])
        for n in range(PLANE)
    ]
    for out in outs:
        out.start()
    for out in outs:
        out.wait()


def pack(place, index, received, copies):
    blocks, width = received.shape[1:]
    half = jax.ShapeDtypeStruct((2 * SHARE, blocks // 2, width), received.dtype)
    return pl.pallas_call(
        pack_kernel,
        out_shape=(half, half, jax.ShapeDtypeStruct((PLANE * 2 * SHARE, width), received.dtype)),
        in_specs=[SMEM, SMEM] + [HBM] * (1 + SIDE),
        out_specs=(HBM,) * 3,
        scratch_shapes=[
            pltpu.VMEM((2 * SHARE, blocks, width), received.dtype),
            pltpu.VMEM((2 * SHARE, width), received.dtype),
            pltpu.SemaphoreType.DMA((SHARE + 1,)),
            pltpu.SemaphoreType.DMA((2 + PLANE,)),
        ],
        compiler_params=SMALL,
        name="pack",
    )(place, index, received, *copies)


def permute(value, pairs):
    return lax.ppermute(value, "prow", pairs)


def along(axis, offset):
    return moves(0, offset, 0) if axis == "y" else moves(0, 0, offset)


def leave_home(block, me):
    held = block[:QUARTER]
    y = me // SIDE % SIDE
    parts = [
        permute(block[QUARTER * n : QUARTER * (n + 1)], [(h, chip(0, n, h)) for h in range(2)])
        for n in range(1, SIDE)
    ]
    for n, part in enumerate(parts):
        held = jnp.where(y == n + 1, part, held)
    return held


def climb(held, me):
    across = permute(held[SHARE:], [(chip(0, n, h), chip(0, n, h + 2)) for n in range(SIDE) for h in range(2)])
    own = jnp.where(me % SIDE < 2, held[:SHARE], across)
    return [own] + [permute(own, [(n, z * PLANE + n) for n in range(PLANE)]) for z in range(1, SIDE)]


def gather_line(value, axis):
    return jnp.concatenate([value] + [permute(value, along(axis, -offset)) for offset in OFFSETS[1:]], axis=0)


def neighbours(line, axis):
    return permute(line, along(axis, 1)), permute(line, along(axis, -1))


def gather_across(line, hops, axis):
    before, after = hops
    half = line.shape[0] // 2
    far_low, far_high = permute(before[:half], along(axis, 1)), permute(after[half:], along(axis, -1))
    return [line, before, after, far_low, far_high]


def dot(left, right):
    return jnp.dot(left, right, precision=lax.Precision.HIGHEST, preferred_element_type=jnp.float32)


def single(left, right):
    return jnp.dot(left, right, preferred_element_type=jnp.float32)


def halves(value):
    high = value.astype(jnp.bfloat16)
    return high, (value - high.astype(jnp.float32)).astype(jnp.bfloat16)


def weigh_kernel(
    place, moved, panel, head, orders, upper_inverse, lower_inverse,
    weights_hbm, edge_hbm, own_panel, weights, edge, sems,
):
    grid_row, grid_column = place[0], place[1]
    own_panel[...] = panel[...]

    def patch(i, carry):
        for side in range(2):
            own_panel[side, pl.ds(moved[i], 1), :] = head[side, pl.ds(moved[3 * PICKS + i], 1), :]
        return carry

    lax.fori_loop(0, moved[4 * PICKS], patch, 0)

    hot = [
        lax.broadcasted_iota(jnp.int32, (PICKS, PICKS), 0) == orders[n : n + 1, :] for n in range(3)
    ]
    row_at = lax.broadcasted_iota(jnp.int32, (NB, NB), 0)
    column_at = lax.broadcasted_iota(jnp.int32, (NB, NB), 1)
    upper = [jnp.where(row_at <= column_at, upper_inverse[k], 0.0) for k in range(2)]
    lower = [
        jnp.where(row_at > column_at, lower_inverse[k], jnp.where(row_at == column_at, 1.0, 0.0))
        for k in range(2)
    ]
    dealt = [
        jnp.concatenate([head[k, 2 * SHARE * n : 2 * SHARE * n + SHARE, :] for n in range(PLANE)], axis=0)
        for k in range(2)
    ]
    picked = dot(hot[2].astype(jnp.float32), jnp.concatenate(dealt, axis=1))
    block_lower = dot(picked[NB:, :NB], upper[0])
    block_upper = dot(lower[0], picked[:NB, NB:])
    block_second = picked[NB:, NB:] - dot(block_lower, block_upper)
    mixed = -dot(lower[1], dot(block_lower, lower[0]))
    lower_first = dot(own_panel[0], upper[0])
    lower_second = dot(own_panel[1] - dot(lower_first, block_upper), upper[1])
    weight_first = dot(lower_first, lower[0]) + dot(lower_second, mixed)
    weight_second = dot(lower_second, lower[1])
    first_home, second_home = grid_row == 0, grid_row == 1

    def at_home(first, second, other):
        top = jnp.where(first_home, first, jnp.where(second_home, second, other[:NB]))
        return jnp.concatenate([top, other[NB:]], axis=0)

    weight = jnp.concatenate(
        [
            at_home(-lower[0], -mixed, weight_first),
            at_home(jnp.zeros_like(lower[1]), -lower[1], weight_second),
        ],
        axis=1,
    )
    high, low = halves(weight)
    for side in range(2):
        place_at = hot[side].astype(jnp.bfloat16)
        weights[2 * side] = single(high, place_at).astype(jnp.bfloat16)
        weights[2 * side + 1] = single(low, place_at).astype(jnp.bfloat16)
    edge[...] = jnp.where(
        grid_column == 0,
        at_home(picked[:NB, :NB], block_lower, lower_first),
        at_home(block_upper, block_second, lower_second),
    )
    outs = [
        pltpu.make_async_copy(weights, weights_hbm, sems.at[0]),
        pltpu.make_async_copy(edge, edge_hbm, sems.at[1]),
    ]
    for out in outs:
        out.start()
    for out in outs:
        out.wait()


def weigh(place, moved, panel, head, orders, upper_inverse, lower_inverse):
    local_rows = panel.shape[1]
    return pl.pallas_call(
        weigh_kernel,
        out_shape=(
            jax.ShapeDtypeStruct((4, local_rows, PICKS), jnp.bfloat16),
            jax.ShapeDtypeStruct((local_rows, NB), jnp.float32),
        ),
        in_specs=[SMEM] * 2 + [VMEM] * 5,
        out_specs=(HBM, HBM),
        scratch_shapes=[
            pltpu.VMEM((2, local_rows, NB), jnp.float32),
            pltpu.VMEM((4, local_rows, PICKS), jnp.bfloat16),
            pltpu.VMEM((local_rows, NB), jnp.float32),
            pltpu.SemaphoreType.DMA((2,)),
        ],
        compiler_params=pltpu.CompilerParams(vmem_limit_bytes=24 << 20),
        cost_estimate=pl.CostEstimate(flops=1_200_000_000, transcendentals=0, bytes_accessed=20_000_000),
        name="weigh",
    )(place, moved, panel, head, orders.reshape(3, PICKS), upper_inverse, lower_inverse)


def update_kernel(*refs):
    place, moved, weights_hbm, edge_hbm, rows_hbm = refs[:5]
    pieces, out_hbm = (refs[5:10], refs[10:15]), refs[15]
    rows, plane, kept, result, weights, edge = refs[16:22]
    row_sems, piece_sems, kept_sems, out_sems, weight_sems = refs[22:]
    groups, half = rows.shape[0], plane.shape[3]
    is_home = place[0] < 2
    found = moved[4 * PICKS]
    begins = (0, 4, 8, 12, 14, 16)

    def fetch_rows(group):
        columns = pl.ds(group * GROUP, GROUP)
        return pltpu.make_async_copy(rows_hbm.at[:, columns, :], rows.at[group], row_sems.at[group])

    def fetch_piece(side, n):
        source = pieces[side][n].at[:, pl.ds(0, SHARE)]
        target = plane.at[side, pl.ds(begins[n], begins[n + 1] - begins[n])]
        return pltpu.make_async_copy(source, target, piece_sems.at[side, n])

    def kept_half(i, side, source):
        return pltpu.make_async_copy(source, kept.at[side, i], kept_sems.at[side, i])

    def start_kept(i, carry):
        for side in range(2):
            at = moved[(1 + side) * PICKS + i]
            there = at // SHARE
            for n, piece in enumerate(pieces[side]):

                @pl.when(jnp.logical_and(there >= begins[n], there < begins[n + 1]))
                def _():
                    chunk = jnp.clip(there - begins[n], 0, begins[n + 1] - begins[n] - 1)
                    kept_half(i, side, piece.at[chunk, SHARE + at % SHARE]).start()

        return carry

    def wait_kept(i, carry):
        for side in range(2):
            kept_half(i, side, pieces[side][0].at[0, 0]).wait()
        return carry

    def write(group, slot):
        return pltpu.make_async_copy(
            result.at[slot], out_hbm.at[:, pl.ds(group * GROUP, GROUP), :], out_sems.at[slot]
        )

    factors = [
        pltpu.make_async_copy(weights_hbm, weights, weight_sems.at[0]),
        pltpu.make_async_copy(edge_hbm, edge, weight_sems.at[1]),
    ]
    for factor in factors:
        factor.start()
    for side in range(2):
        for n in range(5):
            fetch_piece(side, n).start()
        for group in range(side * groups // 2, (side + 1) * groups // 2):
            fetch_rows(group).start()
        if side == 0:
            lax.fori_loop(0, found, start_kept, 0)

    for group in range(groups):
        slot, side = group % 2, group * GROUP // half
        begin = group * GROUP % half
        if begin == 0:
            for n in range(5):
                fetch_piece(side, n).wait()
        if group == 0:
            lax.fori_loop(0, found, wait_kept, 0)
            for factor in factors:
                factor.wait()
        fetch_rows(group).wait()

        def patch(i, carry):
            rows[group, moved[i], :, :] = kept[side, i, begin : begin + GROUP, :]
            return carry

        lax.fori_loop(0, found, patch, 0)
        if group >= 2:
            write(group - 2, slot).wait()
        picked = plane[side, :, :, begin : begin + GROUP, :].reshape(PICKS, GROUP, NB)
        picked = pltpu.einshape("rcl->crl", picked)
        products = []
        for pair in range(GROUP // 2):
            right_high, right_low = halves(jnp.concatenate([picked[2 * pair], picked[2 * pair + 1]], axis=1))
            product = single(weights[2 * side], right_high)
            product += single(weights[2 * side], right_low)
            product += single(weights[2 * side + 1], right_high)
            products += [product[:, :NB], product[:, NB:]]
        product = pltpu.einshape("crl->rcl", jnp.stack(products, axis=0))
        result[slot, :NB] = jnp.where(is_home, 0.0, rows[group, :NB]) - product[:NB]
        result[slot, NB:] = rows[group, NB:] - product[NB:]
        if group == 0:
            result[slot, :, 0, :] = edge[...]
        write(group, slot).start()
    for group in range(max(0, groups - 2), groups):
        write(group, group % 2).wait()


def update(place, moved, weights, edge, rows, pieces):
    local_rows, blocks, _ = rows.shape
    groups = blocks // GROUP
    pieces = [piece.reshape((-1, 2 * SHARE) + piece.shape[1:]) for side in pieces for piece in side]
    return pl.pallas_call(
        update_kernel,
        out_shape=jax.ShapeDtypeStruct(rows.shape, rows.dtype),
        in_specs=[SMEM] * 2 + [HBM] * 13,
        out_specs=HBM,
        scratch_shapes=[
            pltpu.VMEM((groups, local_rows, GROUP, NB), jnp.float32),
            pltpu.VMEM((2, PLANE, SHARE, blocks // 2, NB), jnp.float32),
            pltpu.VMEM((2, PICKS, blocks // 2, NB), jnp.float32),
            pltpu.VMEM((2, local_rows, GROUP, NB), jnp.float32),
            pltpu.VMEM((4, local_rows, PICKS), jnp.bfloat16),
            pltpu.VMEM((local_rows, NB), jnp.float32),
            pltpu.SemaphoreType.DMA((groups,)),
            pltpu.SemaphoreType.DMA((2, 5)),
            pltpu.SemaphoreType.DMA((2, PICKS)),
            pltpu.SemaphoreType.DMA((2,)),
            pltpu.SemaphoreType.DMA((2,)),
        ],
        compiler_params=pltpu.CompilerParams(vmem_limit_bytes=56 << 20),
        cost_estimate=pl.CostEstimate(flops=3_300_000_000, transcendentals=0, bytes_accessed=26_000_000),
        name="update",
    )(place, moved, weights, edge, rows, *pieces)


def local(matrix, pivots, upper_inverse, lower_inverse):
    me = lax.axis_index("prow")
    rows = matrix.reshape(matrix.shape[0] * NB, matrix.shape[3], NB)
    place = jnp.stack([me, lax.axis_index("pcol")]).astype(jnp.int32)
    pivots = pivots.reshape(-1)
    panel = lax.all_gather(rows[:, 0, :], "pcol", axis=0)
    held = leave_home(rows[:NB], me)
    picked, kept = exchange(pivots, rows.shape[0] * SIDE * PLANE)
    rank, most = ranks_of(picked)
    sent, pick_row, hub_source = deal(place, picked, rank, rows)
    received = swap_all(sent)
    copies = climb(held, me)
    moved, orders = tables(place, pivots, kept, rank)
    received, index = lax.cond(
        most <= SHARE,
        lambda: (received, hub_source),
        lambda: crowded(place, pick_row, hub_source, rows, received),
    )
    index, orders = lax.optimization_barrier((index, orders))
    left, right, head = pack(place, index, received, copies)
    planes = [list(range(z * PLANE, (z + 1) * PLANE)) for z in range(SIDE)]
    head = lax.all_to_all(head, "prow", 0, 0, tiled=True, axis_index_groups=planes)
    lines = gather_line(left, "x"), gather_line(right, "y")
    hops = neighbours(lines[0], "y"), neighbours(lines[1], "x")
    *hops, head = lax.optimization_barrier((*hops, head))
    head = lax.all_gather(head, "pcol", axis=0)
    pieces = [gather_across(*parts) for parts in zip(lines, hops, "yx")]
    weights, edge = weigh(place, moved, panel, head, orders, upper_inverse, lower_inverse)
    out = update(place, moved, weights, edge, rows, pieces)
    return out.reshape(matrix.shape)


def solution(mesh):
    return jax.shard_map(
        local,
        mesh=mesh,
        in_specs=(P(None, "prow", None, None, "pcol", None), P(), P(), P()),
        out_specs=P(None, "prow", None, None, "pcol", None),
        check_vma=False,
    )
```

```python
import jax
import jax.numpy as jnp
from jax import lax
from jax.experimental import pallas as pl
from jax.experimental.pallas import tpu as pltpu
from jax.sharding import PartitionSpec as P

NB = 128
PICKS = 2 * NB
SIDE = 4
PLANE = SIDE * SIDE
SHARE = PICKS // PLANE
QUARTER = NB // SIDE
GROUP = 8
OFFSETS = (0, -1, 1, 2)
HBM = pl.BlockSpec(memory_space=pl.ANY)
SMEM = pl.BlockSpec(memory_space=pltpu.SMEM)
VMEM = pl.BlockSpec(memory_space=pltpu.VMEM)
SMALL = pltpu.CompilerParams(vmem_limit_bytes=4 << 20)


def chip(z, y, x):
    return (z % SIDE * SIDE + y % SIDE) * SIDE + x % SIDE


def moves(dz, dy, dx):
    span = range(SIDE)
    return [(chip(z, y, x), chip(z + dz, y + dy, x + dx)) for z in span for y in span for x in span]


def owner_of(row):
    return (row >> 7) & (SIDE * PLANE - 1)


def local_of(row):
    return ((row >> 13) << 7) | (row & (NB - 1))


def each(count, body, unroll=8):
    def step(i, carry):
        body(i)
        return carry

    lax.fori_loop(0, count, step, 0, unroll=unroll)


def exchange_kernel(pivots, picked, kept, source):
    def start(i):
        chosen = pivots[i]
        source[chosen] = chosen
        source[i] = i

    each(PICKS, start)

    def exchange(i):
        chosen = pivots[i]
        at_target = source[i]
        at_chosen = source[chosen]
        source[i] = at_chosen
        source[chosen] = at_target

    each(PICKS, exchange)

    def keep(i):
        picked[i] = source[i]
        kept[i] = source[pivots[i]]

    each(PICKS, keep)


def exchange(pivots, row_count):
    table = jax.ShapeDtypeStruct((PICKS,), jnp.int32)
    return pl.pallas_call(
        exchange_kernel,
        out_shape=(table, table),
        in_specs=[SMEM],
        out_specs=(SMEM, SMEM),
        scratch_shapes=[pltpu.SMEM((row_count,), jnp.int32)],
        cost_estimate=pl.CostEstimate(flops=0, transcendentals=0, bytes_accessed=60_000_000),
        compiler_params=SMALL,
        name="exchange",
    )(pivots)


def ranks_of(picked):
    owner = owner_of(picked)
    earlier = owner[None, :] < owner[:, None]
    same = owner[None, :] == owner[:, None]
    index = jnp.arange(PICKS)
    ahead = jnp.logical_or(earlier, jnp.logical_and(same, index[None, :] < index[:, None]))
    rank = jnp.sum(ahead.astype(jnp.int32), axis=1)
    return rank, jnp.max(jnp.sum(same.astype(jnp.int32), axis=1))


def deal_kernel(
    place, picked, rank, rows_hbm, send_hbm, pick_row, hub_source, own, held, held_sems, sems
):
    me = place[0]

    def note(i, count):
        row = picked[i]
        pick_row[rank[i]] = row
        own[count] = i
        return count + (owner_of(row) == me).astype(jnp.int32)

    count = jnp.minimum(lax.fori_loop(0, PICKS, note, 0, unroll=16), SHARE)

    def fetch(n):
        return pltpu.make_async_copy(rows_hbm.at[local_of(picked[own[n]])], held.at[n], held_sems.at[n])

    def copy_of(n, z):
        column = rank[own[n]] % PLANE
        return pltpu.make_async_copy(held.at[n], send_hbm.at[z * PLANE + column], sems.at[n * SIDE + z])

    def loop(body):
        def step(n, carry):
            body(n)
            return carry

        lax.fori_loop(0, count, step, 0)

    def send(n):
        fetch(n).wait()
        for z in range(SIDE):
            copy_of(n, z).start()

    def finish(n):
        for z in range(SIDE):
            copy_of(n, z).wait()

    def hub(t):
        hub_source[t] = owner_of(pick_row[t * PLANE + me % PLANE])

    loop(lambda n: fetch(n).start())
    each(SHARE, hub, 16)
    loop(send)
    loop(finish)


def deal(place, picked, rank, rows):
    chips = SIDE * PLANE
    return pl.pallas_call(
        deal_kernel,
        out_shape=(
            jax.ShapeDtypeStruct((chips,) + rows.shape[1:], rows.dtype),
            jax.ShapeDtypeStruct((PICKS,), jnp.int32),
            jax.ShapeDtypeStruct((SHARE,), jnp.int32),
        ),
        in_specs=[SMEM, SMEM, SMEM, HBM],
        out_specs=(HBM, SMEM, SMEM),
        scratch_shapes=[
            pltpu.SMEM((PICKS + 1,), jnp.int32),
            pltpu.VMEM((SHARE,) + rows.shape[1:], rows.dtype),
            pltpu.SemaphoreType.DMA((SHARE,)),
            pltpu.SemaphoreType.DMA((SHARE * SIDE,)),
        ],
        cost_estimate=pl.CostEstimate(flops=0, transcendentals=0, bytes_accessed=30_000_000),
        compiler_params=SMALL,
        name="deal",
    )(place, picked, rank, rows)


def table_kernel(place, pivots, kept, rank, moved, orders, order):
    me = place[0]
    my_y, my_x = me // SIDE % SIDE, me % SIDE

    def invert(i):
        order[rank[i]] = i

    each(PICKS, invert, 16)

    def at_offset(there, here):
        apart = (there - here) % SIDE
        return jnp.where(apart == 3, 1, jnp.where(apart == 0, 0, apart + 1))

    def list_moved(i, count):
        chosen = pivots[i]
        moved[count] = i
        is_mine = jnp.logical_and(owner_of(chosen) == me, chosen >= PICKS)
        return count + is_mine.astype(jnp.int32)

    count = lax.fori_loop(0, PICKS, list_moved, 0, unroll=16)
    moved[4 * PICKS] = count

    def name_moved(n, carry):
        i = moved[n]
        home, held = kept[i] // NB, kept[i] % NB
        x, y, t = home + 2 * (held % QUARTER // SHARE), held // QUARTER, held % SHARE
        at_x, at_y = at_offset(x, my_x), at_offset(y, my_y)
        moved[n] = local_of(pivots[i])
        moved[PICKS + n] = (at_y * SIDE + at_x) * SHARE + t
        moved[2 * PICKS + n] = (at_x * SIDE + at_y) * SHARE + t
        moved[3 * PICKS + n] = (y * SIDE + x) * 2 * SHARE + SHARE + t
        return carry

    lax.fori_loop(0, count, name_moved, 0)

    for a, dy in enumerate(OFFSETS):
        for b, dx in enumerate(OFFSETS):
            column = (my_y + dy) % SIDE * SIDE + (my_x + dx) % SIDE
            for t in range(SHARE):
                pick = order[t * PLANE + column]
                orders[(a * SIDE + b) * SHARE + t] = pick
                orders[PICKS + (b * SIDE + a) * SHARE + t] = pick
                orders[2 * PICKS + column * SHARE + t] = pick


def tables(place, pivots, kept, rank):
    return pl.pallas_call(
        table_kernel,
        out_shape=[jax.ShapeDtypeStruct((n,), jnp.int32) for n in (4 * PICKS + 1, 3 * PICKS)],
        in_specs=[SMEM] * 4,
        out_specs=[SMEM] * 2,
        scratch_shapes=[pltpu.SMEM((PICKS,), jnp.int32)],
        cost_estimate=pl.CostEstimate(flops=0, transcendentals=0, bytes_accessed=20_000_000),
        compiler_params=SMALL,
        name="tables",
    )(place, pivots, kept, rank)


def round_kernel(at, place, pick_row, rows_hbm, send_hbm, sems):
    me = place[0]

    def copy_of(h, z):
        row = pick_row[at[0] * PLANE + h]
        copy = pltpu.make_async_copy(
            rows_hbm.at[local_of(row)], send_hbm.at[z * PLANE + h], sems.at[h * SIDE + z]
        )
        return owner_of(row) == me, copy

    def go(h):
        for z in range(SIDE):
            held, copy = copy_of(h, z)
            pl.when(held)(copy.start)

    each(PLANE, go, 1)

    def finish(h):
        for z in range(SIDE):
            held, copy = copy_of(h, z)
            pl.when(held)(copy.wait)

    each(PLANE, finish, 1)


def send_round(at, place, pick_row, rows):
    return pl.pallas_call(
        round_kernel,
        out_shape=jax.ShapeDtypeStruct((SIDE * PLANE,) + rows.shape[1:], rows.dtype),
        in_specs=[SMEM, SMEM, SMEM, HBM],
        out_specs=HBM,
        scratch_shapes=[pltpu.SemaphoreType.DMA((PLANE * SIDE,))],
        compiler_params=SMALL,
        name="send_round",
    )(at, place, pick_row, rows)


def swap_all(rows):
    return lax.all_to_all(rows, "prow", 0, 0, tiled=True)


def crowded(place, pick_row, hub_source, rows):
    def step(t, held):
        sent = send_round(jnp.full((1,), t, jnp.int32), place, pick_row, rows)
        row = lax.dynamic_slice_in_dim(swap_all(sent), hub_source[t], 1, axis=0)
        return lax.dynamic_update_slice_in_dim(held, row, t, axis=0)

    return lax.fori_loop(0, SHARE, step, jnp.zeros((SHARE,) + rows.shape[1:], rows.dtype))


def pack_kernel(place, index, received, spare, *refs):
    copies, left, right, heads, buffer, edge, sems, out_sems = refs[:SIDE], *refs[SIDE:]
    z = place[0] // PLANE

    def pick(t):
        return pltpu.make_async_copy(received.at[jnp.maximum(index[t], 0)], buffer.at[t], sems.at[t])

    def previous(held):
        return pltpu.make_async_copy(held, buffer.at[pl.ds(SHARE, SHARE)], sems.at[SHARE])

    balanced = index[0] >= 0
    pl.when(balanced)(lambda: each(SHARE, lambda t: pick(t).start()))

    @pl.when(jnp.logical_not(balanced))
    def _():
        whole = pltpu.make_async_copy(spare, buffer.at[pl.ds(0, SHARE)], sems.at[0])
        whole.start()
        whole.wait()

    for level, held in enumerate(copies):
        pl.when(z == level)(lambda held=held: previous(held).start())
    pl.when(balanced)(lambda: each(SHARE, lambda t: pick(t).wait()))
    previous(copies[0]).wait()
    edge[...] = buffer[:, 0, :]
    half = left.shape[1]
    outs = [
        pltpu.make_async_copy(buffer.at[:, pl.ds(n * half, half), :], out, out_sems.at[n])
        for n, out in enumerate((left, right))
    ]
    outs += [
        pltpu.make_async_copy(edge, heads.at[pl.ds(n * 2 * SHARE, 2 * SHARE)], out_sems.at[2 + n])
        for n in range(PLANE)
    ]
    for out in outs:
        out.start()
    for out in outs:
        out.wait()


def pack(place, index, received, spare, copies):
    blocks, width = received.shape[1:]
    half = jax.ShapeDtypeStruct((2 * SHARE, blocks // 2, width), received.dtype)
    return pl.pallas_call(
        pack_kernel,
        out_shape=(half, half, jax.ShapeDtypeStruct((PLANE * 2 * SHARE, width), received.dtype)),
        in_specs=[SMEM, SMEM] + [HBM] * (2 + SIDE),
        out_specs=(HBM,) * 3,
        scratch_shapes=[
            pltpu.VMEM((2 * SHARE, blocks, width), received.dtype),
            pltpu.VMEM((2 * SHARE, width), received.dtype),
            pltpu.SemaphoreType.DMA((SHARE + 1,)),
            pltpu.SemaphoreType.DMA((2 + PLANE,)),
        ],
        compiler_params=SMALL,
        name="pack",
    )(place, index, received, spare, *copies)


def permute(value, pairs):
    return lax.ppermute(value, "prow", pairs)


def along(axis, offset):
    return moves(0, offset, 0) if axis == "y" else moves(0, 0, offset)


def leave_home(block, me):
    held = block[:QUARTER]
    y = me // SIDE % SIDE
    parts = [
        permute(block[QUARTER * n : QUARTER * (n + 1)], [(h, chip(0, n, h)) for h in range(2)])
        for n in range(1, SIDE)
    ]
    for n, part in enumerate(parts):
        held = jnp.where(y == n + 1, part, held)
    return held


def climb(held, me):
    across = permute(held[SHARE:], [(chip(0, n, h), chip(0, n, h + 2)) for n in range(SIDE) for h in range(2)])
    own = jnp.where(me % SIDE < 2, held[:SHARE], across)
    return [own] + [permute(own, [(n, z * PLANE + n) for n in range(PLANE)]) for z in range(1, SIDE)]


def gather_line(value, axis):
    return jnp.concatenate([value] + [permute(value, along(axis, -offset)) for offset in OFFSETS[1:]], axis=0)


def neighbours(line, axis):
    return permute(line, along(axis, 1)), permute(line, along(axis, -1))


def gather_across(line, hops, axis):
    before, after = hops
    half = line.shape[0] // 2
    far_low, far_high = permute(before[:half], along(axis, 1)), permute(after[half:], along(axis, -1))
    return [line, before, after, far_low, far_high]


def dot(left, right):
    return jnp.dot(left, right, precision=lax.Precision.HIGHEST, preferred_element_type=jnp.float32)


def single(left, right):
    return jnp.dot(left, right, preferred_element_type=jnp.float32)


def halves(value):
    high = value.astype(jnp.bfloat16)
    return high, (value - high.astype(jnp.float32)).astype(jnp.bfloat16)


def weigh_kernel(
    place, moved, panel, head, orders, upper_inverse, lower_inverse,
    weights_hbm, edge_hbm, own_panel, weights, edge, sems,
):
    grid_row, grid_column = place[0], place[1]
    own_panel[...] = panel[...]

    def patch(i, carry):
        for side in range(2):
            own_panel[side, pl.ds(moved[i], 1), :] = head[side, pl.ds(moved[3 * PICKS + i], 1), :]
        return carry

    lax.fori_loop(0, moved[4 * PICKS], patch, 0)

    hot = [
        lax.broadcasted_iota(jnp.int32, (PICKS, PICKS), 0) == orders[n : n + 1, :] for n in range(3)
    ]
    row_at = lax.broadcasted_iota(jnp.int32, (NB, NB), 0)
    column_at = lax.broadcasted_iota(jnp.int32, (NB, NB), 1)
    upper = [jnp.where(row_at <= column_at, upper_inverse[k], 0.0) for k in range(2)]
    lower = [
        jnp.where(row_at > column_at, lower_inverse[k], jnp.where(row_at == column_at, 1.0, 0.0))
        for k in range(2)
    ]
    dealt = [
        jnp.concatenate([head[k, 2 * SHARE * n : 2 * SHARE * n + SHARE, :] for n in range(PLANE)], axis=0)
        for k in range(2)
    ]
    picked = dot(hot[2].astype(jnp.float32), jnp.concatenate(dealt, axis=1))
    block_lower = dot(picked[NB:, :NB], upper[0])
    block_upper = dot(lower[0], picked[:NB, NB:])
    block_second = picked[NB:, NB:] - dot(block_lower, block_upper)
    mixed = -dot(lower[1], dot(block_lower, lower[0]))
    lower_first = dot(own_panel[0], upper[0])
    lower_second = dot(own_panel[1] - dot(lower_first, block_upper), upper[1])
    weight_first = dot(lower_first, lower[0]) + dot(lower_second, mixed)
    weight_second = dot(lower_second, lower[1])
    first_home, second_home = grid_row == 0, grid_row == 1

    def at_home(first, second, other):
        top = jnp.where(first_home, first, jnp.where(second_home, second, other[:NB]))
        return jnp.concatenate([top, other[NB:]], axis=0)

    weight = jnp.concatenate(
        [
            at_home(-lower[0], -mixed, weight_first),
            at_home(jnp.zeros_like(lower[1]), -lower[1], weight_second),
        ],
        axis=1,
    )
    high, low = halves(weight)
    for side in range(2):
        place_at = hot[side].astype(jnp.bfloat16)
        weights[2 * side] = single(high, place_at).astype(jnp.bfloat16)
        weights[2 * side + 1] = single(low, place_at).astype(jnp.bfloat16)
    edge[...] = jnp.where(
        grid_column == 0,
        at_home(picked[:NB, :NB], block_lower, lower_first),
        at_home(block_upper, block_second, lower_second),
    )
    outs = [
        pltpu.make_async_copy(weights, weights_hbm, sems.at[0]),
        pltpu.make_async_copy(edge, edge_hbm, sems.at[1]),
    ]
    for out in outs:
        out.start()
    for out in outs:
        out.wait()


def weigh(place, moved, panel, head, orders, upper_inverse, lower_inverse):
    local_rows = panel.shape[1]
    return pl.pallas_call(
        weigh_kernel,
        out_shape=(
            jax.ShapeDtypeStruct((4, local_rows, PICKS), jnp.bfloat16),
            jax.ShapeDtypeStruct((local_rows, NB), jnp.float32),
        ),
        in_specs=[SMEM] * 2 + [VMEM] * 5,
        out_specs=(HBM, HBM),
        scratch_shapes=[
            pltpu.VMEM((2, local_rows, NB), jnp.float32),
            pltpu.VMEM((4, local_rows, PICKS), jnp.bfloat16),
            pltpu.VMEM((local_rows, NB), jnp.float32),
            pltpu.SemaphoreType.DMA((2,)),
        ],
        compiler_params=pltpu.CompilerParams(vmem_limit_bytes=61 << 20),
        cost_estimate=pl.CostEstimate(flops=1_200_000_000, transcendentals=0, bytes_accessed=20_000_000),
        name="weigh",
    )(place, moved, panel, head, orders.reshape(3, PICKS), upper_inverse, lower_inverse)


def update_kernel(*refs):
    place, moved, weights_hbm, edge_hbm, rows_hbm = refs[:5]
    pieces, out_hbm = (refs[5:10], refs[10:15]), refs[15]
    rows, plane, result, weights, edge = refs[16:21]
    row_sems, piece_sems, out_sems, weight_sems = refs[21:]
    groups, half = rows.shape[0], plane.shape[3]
    is_home = place[0] < 2
    found = moved[4 * PICKS]
    begins = (0, 4, 8, 12, 14, 16)

    def fetch_rows(group):
        columns = pl.ds(group * GROUP, GROUP)
        return pltpu.make_async_copy(rows_hbm.at[:, columns, :], rows.at[group], row_sems.at[group])

    def fetch_piece(side, n, kind):
        count = begins[n + 1] - begins[n]
        part = pl.ds(kind * SHARE, SHARE)
        return pltpu.make_async_copy(
            pieces[side][n].at[:, part],
            plane.at[side, pl.ds(begins[n], count), part],
            piece_sems.at[side, n, kind],
        )

    def write(group, slot):
        return pltpu.make_async_copy(
            result.at[slot], out_hbm.at[:, pl.ds(group * GROUP, GROUP), :], out_sems.at[slot]
        )

    factors = [
        pltpu.make_async_copy(weights_hbm, weights, weight_sems.at[0]),
        pltpu.make_async_copy(edge_hbm, edge, weight_sems.at[1]),
    ]
    for factor in factors:
        factor.start()
    def start_pieces(side, kind):
        for n in range(5):
            fetch_piece(side, n, kind).start()

    start_pieces(0, 0)
    fetch_rows(0).start()
    start_pieces(0, 1)
    fetch_rows(1).start()

    for group in range(groups):
        slot, side = group % 2, group * GROUP // half
        begin = group * GROUP % half
        if begin == 0:
            for n in range(5):
                fetch_piece(side, n, 0).wait()
        if group == 0:
            for factor in factors:
                factor.wait()
            start_pieces(1, 0)
            start_pieces(1, 1)
        if group + 2 < groups:
            fetch_rows(group + 2).start()
        if group >= 2:
            write(group - 2, slot).wait()
        picked = plane[side, :, :SHARE, begin : begin + GROUP, :].reshape(PICKS, GROUP, NB)
        picked = pltpu.einshape("rcl->crl", picked)
        products = []
        for pair in range(GROUP // 2):
            right_high, right_low = halves(jnp.concatenate([picked[2 * pair], picked[2 * pair + 1]], axis=1))
            product = single(weights[2 * side], right_high)
            product += single(weights[2 * side], right_low)
            product += single(weights[2 * side + 1], right_high)
            products += [product[:, :NB], product[:, NB:]]
        product = pltpu.einshape("crl->rcl", jnp.stack(products, axis=0))
        if begin == 0:
            for n in range(5):
                fetch_piece(side, n, 1).wait()
        fetch_rows(group).wait()

        def patch(i, carry):
            at = moved[(1 + side) * PICKS + i]
            rows[group, moved[i], :, :] = plane[side, at // SHARE, SHARE + at % SHARE, begin : begin + GROUP, :]
            return carry

        lax.fori_loop(0, found, patch, 0)
        result[slot, :NB] = jnp.where(is_home, 0.0, rows[group, :NB]) - product[:NB]
        result[slot, NB:] = rows[group, NB:] - product[NB:]
        if group == 0:
            result[slot, :, 0, :] = edge[...]
        write(group, slot).start()
    for group in range(max(0, groups - 2), groups):
        write(group, group % 2).wait()


def update(place, moved, weights, edge, rows, pieces):
    local_rows, blocks, _ = rows.shape
    groups = blocks // GROUP
    pieces = [piece.reshape((-1, 2 * SHARE) + piece.shape[1:]) for side in pieces for piece in side]
    return pl.pallas_call(
        update_kernel,
        out_shape=jax.ShapeDtypeStruct(rows.shape, rows.dtype),
        in_specs=[SMEM] * 2 + [HBM] * 13,
        out_specs=HBM,
        scratch_shapes=[
            pltpu.VMEM((groups, local_rows, GROUP, NB), jnp.float32),
            pltpu.VMEM((2, PLANE, 2 * SHARE, blocks // 2, NB), jnp.float32),
            pltpu.VMEM((2, local_rows, GROUP, NB), jnp.float32),
            pltpu.VMEM((4, local_rows, PICKS), jnp.bfloat16),
            pltpu.VMEM((local_rows, NB), jnp.float32),
            pltpu.SemaphoreType.DMA((groups,)),
            pltpu.SemaphoreType.DMA((2, 5, 2)),
            pltpu.SemaphoreType.DMA((2,)),
            pltpu.SemaphoreType.DMA((2,)),
        ],
        compiler_params=pltpu.CompilerParams(vmem_limit_bytes=56 << 20),
        cost_estimate=pl.CostEstimate(flops=3_300_000_000, transcendentals=0, bytes_accessed=26_000_000),
        name="update",
    )(place, moved, weights, edge, rows, *pieces)


def local(matrix, pivots, upper_inverse, lower_inverse):
    me = lax.axis_index("prow")
    rows = matrix.reshape(matrix.shape[0] * NB, matrix.shape[3], NB)
    place = jnp.stack([me, lax.axis_index("pcol")]).astype(jnp.int32)
    pivots = pivots.reshape(-1)
    panel = lax.all_gather(rows[:, 0, :], "pcol", axis=0)
    held = leave_home(rows[:NB], me)
    picked, kept = exchange(pivots, rows.shape[0] * SIDE * PLANE)
    rank, most = ranks_of(picked)
    sent, pick_row, hub_source = deal(place, picked, rank, rows)
    received = swap_all(sent)
    held, panel = lax.optimization_barrier((held, panel))
    copies = climb(held, me)
    moved, orders = tables(place, pivots, kept, rank)
    spare = lax.cond(
        most <= SHARE,
        lambda: jnp.zeros((SHARE,) + rows.shape[1:], rows.dtype),
        lambda: crowded(place, pick_row, hub_source, rows),
    )
    index = jnp.where(most <= SHARE, hub_source, -1)
    index, orders = lax.optimization_barrier((index, orders))
    left, right, head = pack(place, index, received, spare, copies)
    planes = [list(range(z * PLANE, (z + 1) * PLANE)) for z in range(SIDE)]
    head = lax.all_to_all(head, "prow", 0, 0, tiled=True, axis_index_groups=planes)
    lines = gather_line(left, "x"), gather_line(right, "y")
    hops = neighbours(lines[0], "y"), neighbours(lines[1], "x")
    *hops, head = lax.optimization_barrier((*hops, head))
    head = lax.all_gather(head, "pcol", axis=0)
    pieces = [gather_across(*parts) for parts in zip(lines, hops, "yx")]
    weights, edge = weigh(place, moved, panel, head, orders, upper_inverse, lower_inverse)
    out = update(place, moved, weights, edge, rows, pieces)
    return out.reshape(matrix.shape)


def solution(mesh):
    return jax.shard_map(
        local,
        mesh=mesh,
        in_specs=(P(None, "prow", None, None, "pcol", None), P(), P(), P()),
        out_specs=P(None, "prow", None, None, "pcol", None),
        check_vma=False,
    )
```

```python
import jax
import jax.numpy as jnp
from jax import lax
from jax.experimental import pallas as pl
from jax.experimental.pallas import tpu as pltpu
from jax.sharding import PartitionSpec as P

NB = 128
PICKS = 2 * NB
SIDE = 4
PLANE = SIDE * SIDE
SHARE = PICKS // PLANE
QUARTER = NB // SIDE
GROUP = 8
OFFSETS = (0, -1, 1, 2)
HBM = pl.BlockSpec(memory_space=pl.ANY)
SMEM = pl.BlockSpec(memory_space=pltpu.SMEM)
VMEM = pl.BlockSpec(memory_space=pltpu.VMEM)
SMALL = pltpu.CompilerParams(vmem_limit_bytes=4 << 20)


def chip(z, y, x):
    return (z % SIDE * SIDE + y % SIDE) * SIDE + x % SIDE


def moves(dz, dy, dx):
    span = range(SIDE)
    return [(chip(z, y, x), chip(z + dz, y + dy, x + dx)) for z in span for y in span for x in span]


def owner_of(row):
    return (row >> 7) & (SIDE * PLANE - 1)


def local_of(row):
    return ((row >> 13) << 7) | (row & (NB - 1))


def each(count, body, unroll=8):
    def step(i, carry):
        body(i)
        return carry

    lax.fori_loop(0, count, step, 0, unroll=unroll)


def exchange_kernel(pivots, picked, kept, source):
    def start(i):
        chosen = pivots[i]
        source[chosen] = chosen
        source[i] = i

    each(PICKS, start)

    def exchange(i):
        chosen = pivots[i]
        at_target = source[i]
        at_chosen = source[chosen]
        source[i] = at_chosen
        source[chosen] = at_target

    each(PICKS, exchange)

    def keep(i):
        picked[i] = source[i]
        kept[i] = source[pivots[i]]

    each(PICKS, keep)


def exchange(pivots, row_count):
    table = jax.ShapeDtypeStruct((PICKS,), jnp.int32)
    return pl.pallas_call(
        exchange_kernel,
        out_shape=(table, table),
        in_specs=[SMEM],
        out_specs=(SMEM, SMEM),
        scratch_shapes=[pltpu.SMEM((row_count,), jnp.int32)],
        cost_estimate=pl.CostEstimate(flops=0, transcendentals=0, bytes_accessed=60_000_000),
        compiler_params=SMALL,
        name="exchange",
    )(pivots)


def ranks_of(picked):
    owner = owner_of(picked)
    earlier = owner[None, :] < owner[:, None]
    same = owner[None, :] == owner[:, None]
    index = jnp.arange(PICKS)
    ahead = jnp.logical_or(earlier, jnp.logical_and(same, index[None, :] < index[:, None]))
    rank = jnp.sum(ahead.astype(jnp.int32), axis=1)
    return rank, jnp.max(jnp.sum(same.astype(jnp.int32), axis=1))


def deal_kernel(
    place, picked, rank, rows_hbm, send_hbm, pick_row, hub_source, own, held, held_sems, sems
):
    me = place[0]

    def note(i, count):
        row = picked[i]
        pick_row[rank[i]] = row
        own[count] = i
        return count + (owner_of(row) == me).astype(jnp.int32)

    count = jnp.minimum(lax.fori_loop(0, PICKS, note, 0, unroll=16), SHARE)

    def fetch(n):
        return pltpu.make_async_copy(rows_hbm.at[local_of(picked[own[n]])], held.at[n], held_sems.at[n])

    def copy_of(n, z):
        column = rank[own[n]] % PLANE
        return pltpu.make_async_copy(held.at[n], send_hbm.at[z * PLANE + column], sems.at[n * SIDE + z])

    def loop(body):
        def step(n, carry):
            body(n)
            return carry

        lax.fori_loop(0, count, step, 0)

    def send(n):
        fetch(n).wait()
        for z in range(SIDE):
            copy_of(n, z).start()

    def finish(n):
        for z in range(SIDE):
            copy_of(n, z).wait()

    def hub(t):
        hub_source[t] = owner_of(pick_row[t * PLANE + me % PLANE])

    loop(lambda n: fetch(n).start())
    each(SHARE, hub, 16)
    loop(send)
    loop(finish)


def deal(place, picked, rank, rows):
    chips = SIDE * PLANE
    return pl.pallas_call(
        deal_kernel,
        out_shape=(
            jax.ShapeDtypeStruct((chips,) + rows.shape[1:], rows.dtype),
            jax.ShapeDtypeStruct((PICKS,), jnp.int32),
            jax.ShapeDtypeStruct((SHARE,), jnp.int32),
        ),
        in_specs=[SMEM, SMEM, SMEM, HBM],
        out_specs=(HBM, SMEM, SMEM),
        scratch_shapes=[
            pltpu.SMEM((PICKS + 1,), jnp.int32),
            pltpu.VMEM((SHARE,) + rows.shape[1:], rows.dtype),
            pltpu.SemaphoreType.DMA((SHARE,)),
            pltpu.SemaphoreType.DMA((SHARE * SIDE,)),
        ],
        cost_estimate=pl.CostEstimate(flops=0, transcendentals=0, bytes_accessed=30_000_000),
        compiler_params=SMALL,
        name="deal",
    )(place, picked, rank, rows)


def table_kernel(place, pivots, kept, rank, moved, orders, order):
    me = place[0]
    my_y, my_x = me // SIDE % SIDE, me % SIDE

    def invert(i):
        order[rank[i]] = i

    each(PICKS, invert, 16)

    def at_offset(there, here):
        apart = (there - here) % SIDE
        return jnp.where(apart == 3, 1, jnp.where(apart == 0, 0, apart + 1))

    def list_moved(i, count):
        chosen = pivots[i]
        moved[count] = i
        is_mine = jnp.logical_and(owner_of(chosen) == me, chosen >= PICKS)
        return count + is_mine.astype(jnp.int32)

    count = lax.fori_loop(0, PICKS, list_moved, 0, unroll=16)
    moved[4 * PICKS] = count

    def name_moved(n, carry):
        i = moved[n]
        home, held = kept[i] // NB, kept[i] % NB
        x, y, t = home + 2 * (held % QUARTER // SHARE), held // QUARTER, held % SHARE
        at_x, at_y = at_offset(x, my_x), at_offset(y, my_y)
        moved[n] = local_of(pivots[i])
        moved[PICKS + n] = (at_y * SIDE + at_x) * SHARE + t
        moved[2 * PICKS + n] = (at_x * SIDE + at_y) * SHARE + t
        moved[3 * PICKS + n] = (y * SIDE + x) * 2 * SHARE + SHARE + t
        return carry

    lax.fori_loop(0, count, name_moved, 0)

    for a, dy in enumerate(OFFSETS):
        for b, dx in enumerate(OFFSETS):
            column = (my_y + dy) % SIDE * SIDE + (my_x + dx) % SIDE
            for t in range(SHARE):
                pick = order[t * PLANE + column]
                orders[(a * SIDE + b) * SHARE + t] = pick
                orders[PICKS + (b * SIDE + a) * SHARE + t] = pick
                orders[2 * PICKS + column * SHARE + t] = pick


def tables(place, pivots, kept, rank):
    return pl.pallas_call(
        table_kernel,
        out_shape=[jax.ShapeDtypeStruct((n,), jnp.int32) for n in (4 * PICKS + 1, 3 * PICKS)],
        in_specs=[SMEM] * 4,
        out_specs=[SMEM] * 2,
        scratch_shapes=[pltpu.SMEM((PICKS,), jnp.int32)],
        cost_estimate=pl.CostEstimate(flops=0, transcendentals=0, bytes_accessed=20_000_000),
        compiler_params=SMALL,
        name="tables",
    )(place, pivots, kept, rank)


def round_kernel(at, place, pick_row, rows_hbm, send_hbm, sems):
    me = place[0]

    def copy_of(h, z):
        row = pick_row[at[0] * PLANE + h]
        copy = pltpu.make_async_copy(
            rows_hbm.at[local_of(row)], send_hbm.at[z * PLANE + h], sems.at[h * SIDE + z]
        )
        return owner_of(row) == me, copy

    def go(h):
        for z in range(SIDE):
            held, copy = copy_of(h, z)
            pl.when(held)(copy.start)

    each(PLANE, go, 1)

    def finish(h):
        for z in range(SIDE):
            held, copy = copy_of(h, z)
            pl.when(held)(copy.wait)

    each(PLANE, finish, 1)


def send_round(at, place, pick_row, rows):
    return pl.pallas_call(
        round_kernel,
        out_shape=jax.ShapeDtypeStruct((SIDE * PLANE,) + rows.shape[1:], rows.dtype),
        in_specs=[SMEM, SMEM, SMEM, HBM],
        out_specs=HBM,
        scratch_shapes=[pltpu.SemaphoreType.DMA((PLANE * SIDE,))],
        compiler_params=SMALL,
        name="send_round",
    )(at, place, pick_row, rows)


def swap_all(rows):
    return lax.all_to_all(rows, "prow", 0, 0, tiled=True)


def crowded(place, pick_row, hub_source, rows):
    def step(t, held):
        sent = send_round(jnp.full((1,), t, jnp.int32), place, pick_row, rows)
        row = lax.dynamic_slice_in_dim(swap_all(sent), hub_source[t], 1, axis=0)
        return lax.dynamic_update_slice_in_dim(held, row, t, axis=0)

    return lax.fori_loop(0, SHARE, step, jnp.zeros((SHARE,) + rows.shape[1:], rows.dtype))


def pack_kernel(place, index, received, spare, *refs):
    copies, left, right, heads, buffer, edge, sems, out_sems = refs[:SIDE], *refs[SIDE:]
    z = place[0] // PLANE

    def pick(t):
        return pltpu.make_async_copy(received.at[jnp.maximum(index[t], 0)], buffer.at[t], sems.at[t])

    def previous(held):
        return pltpu.make_async_copy(held, buffer.at[pl.ds(SHARE, SHARE)], sems.at[SHARE])

    balanced = index[0] >= 0
    pl.when(balanced)(lambda: each(SHARE, lambda t: pick(t).start()))

    @pl.when(jnp.logical_not(balanced))
    def _():
        whole = pltpu.make_async_copy(spare, buffer.at[pl.ds(0, SHARE)], sems.at[0])
        whole.start()
        whole.wait()

    for level, held in enumerate(copies):
        pl.when(z == level)(lambda held=held: previous(held).start())
    pl.when(balanced)(lambda: each(SHARE, lambda t: pick(t).wait()))
    previous(copies[0]).wait()
    edge[...] = buffer[:, 0, :]
    half = left.shape[1]
    outs = [
        pltpu.make_async_copy(buffer.at[:, pl.ds(n * half, half), :], out, out_sems.at[n])
        for n, out in enumerate((left, right))
    ]
    outs += [
        pltpu.make_async_copy(edge, heads.at[pl.ds(n * 2 * SHARE, 2 * SHARE)], out_sems.at[2 + n])
        for n in range(PLANE)
    ]
    for out in outs:
        out.start()
    for out in outs:
        out.wait()


def pack(place, index, received, spare, copies):
    blocks, width = received.shape[1:]
    half = jax.ShapeDtypeStruct((2 * SHARE, blocks // 2, width), received.dtype)
    return pl.pallas_call(
        pack_kernel,
        out_shape=(half, half, jax.ShapeDtypeStruct((PLANE * 2 * SHARE, width), received.dtype)),
        in_specs=[SMEM, SMEM] + [HBM] * (2 + SIDE),
        out_specs=(HBM,) * 3,
        scratch_shapes=[
            pltpu.VMEM((2 * SHARE, blocks, width), received.dtype),
            pltpu.VMEM((2 * SHARE, width), received.dtype),
            pltpu.SemaphoreType.DMA((SHARE + 1,)),
            pltpu.SemaphoreType.DMA((2 + PLANE,)),
        ],
        compiler_params=SMALL,
        name="pack",
    )(place, index, received, spare, *copies)


def permute(value, pairs):
    return lax.ppermute(value, "prow", pairs)


def along(axis, offset):
    return moves(0, offset, 0) if axis == "y" else moves(0, 0, offset)


def leave_home(block, me):
    held = block[:QUARTER]
    y = me // SIDE % SIDE
    parts = [
        permute(block[QUARTER * n : QUARTER * (n + 1)], [(h, chip(0, n, h)) for h in range(2)])
        for n in range(1, SIDE)
    ]
    for n, part in enumerate(parts):
        held = jnp.where(y == n + 1, part, held)
    return held


def climb(held, me, panel):
    across = permute(held[SHARE:], [(chip(0, n, h), chip(0, n, h + 2)) for n in range(SIDE) for h in range(2)])
    across, panel = lax.optimization_barrier((across, panel))
    own = jnp.where(me % SIDE < 2, held[:SHARE], across)
    return [own] + [permute(own, [(n, z * PLANE + n) for n in range(PLANE)]) for z in range(1, SIDE)], panel


def gather_line(value, axis):
    return jnp.concatenate([value] + [permute(value, along(axis, -offset)) for offset in OFFSETS[1:]], axis=0)


def neighbours(line, axis):
    return permute(line, along(axis, 1)), permute(line, along(axis, -1))


def gather_across(line, hops, axis):
    before, after = hops
    half = line.shape[0] // 2
    far_low, far_high = permute(before[:half], along(axis, 1)), permute(after[half:], along(axis, -1))
    return [line, before, after, far_low, far_high]


def dot(left, right):
    return jnp.dot(left, right, precision=lax.Precision.HIGHEST, preferred_element_type=jnp.float32)


def single(left, right):
    return jnp.dot(left, right, preferred_element_type=jnp.float32)


def halves(value):
    high = value.astype(jnp.bfloat16)
    return high, (value - high.astype(jnp.float32)).astype(jnp.bfloat16)


def weigh_kernel(
    place, moved, panel, head, orders, upper_inverse, lower_inverse,
    weights_hbm, edge_hbm, own_panel, weights, edge, sems,
):
    grid_row, grid_column = place[0], place[1]
    own_panel[...] = panel[...]

    def patch(i, carry):
        for side in range(2):
            own_panel[side, pl.ds(moved[i], 1), :] = head[side, pl.ds(moved[3 * PICKS + i], 1), :]
        return carry

    lax.fori_loop(0, moved[4 * PICKS], patch, 0)

    hot = [
        lax.broadcasted_iota(jnp.int32, (PICKS, PICKS), 0) == orders[n : n + 1, :] for n in range(3)
    ]
    row_at = lax.broadcasted_iota(jnp.int32, (NB, NB), 0)
    column_at = lax.broadcasted_iota(jnp.int32, (NB, NB), 1)
    upper = [jnp.where(row_at <= column_at, upper_inverse[k], 0.0) for k in range(2)]
    lower = [
        jnp.where(row_at > column_at, lower_inverse[k], jnp.where(row_at == column_at, 1.0, 0.0))
        for k in range(2)
    ]
    dealt = [
        jnp.concatenate([head[k, 2 * SHARE * n : 2 * SHARE * n + SHARE, :] for n in range(PLANE)], axis=0)
        for k in range(2)
    ]
    picked = dot(hot[2].astype(jnp.float32), jnp.concatenate(dealt, axis=1))
    block_lower = dot(picked[NB:, :NB], upper[0])
    block_upper = dot(lower[0], picked[:NB, NB:])
    block_second = picked[NB:, NB:] - dot(block_lower, block_upper)
    mixed = -dot(lower[1], dot(block_lower, lower[0]))
    lower_first = dot(own_panel[0], upper[0])
    lower_second = dot(own_panel[1] - dot(lower_first, block_upper), upper[1])
    weight_first = dot(lower_first, lower[0]) + dot(lower_second, mixed)
    weight_second = dot(lower_second, lower[1])
    first_home, second_home = grid_row == 0, grid_row == 1

    def at_home(first, second, other):
        top = jnp.where(first_home, first, jnp.where(second_home, second, other[:NB]))
        return jnp.concatenate([top, other[NB:]], axis=0)

    weight = jnp.concatenate(
        [
            at_home(-lower[0], -mixed, weight_first),
            at_home(jnp.zeros_like(lower[1]), -lower[1], weight_second),
        ],
        axis=1,
    )
    high, low = halves(weight)
    for side in range(2):
        place_at = hot[side].astype(jnp.bfloat16)
        weights[2 * side] = single(high, place_at).astype(jnp.bfloat16)
        weights[2 * side + 1] = single(low, place_at).astype(jnp.bfloat16)
    edge[...] = jnp.where(
        grid_column == 0,
        at_home(picked[:NB, :NB], block_lower, lower_first),
        at_home(block_upper, block_second, lower_second),
    )
    outs = [
        pltpu.make_async_copy(weights, weights_hbm, sems.at[0]),
        pltpu.make_async_copy(edge, edge_hbm, sems.at[1]),
    ]
    for out in outs:
        out.start()
    for out in outs:
        out.wait()


def weigh(place, moved, panel, head, orders, upper_inverse, lower_inverse):
    local_rows = panel.shape[1]
    return pl.pallas_call(
        weigh_kernel,
        out_shape=(
            jax.ShapeDtypeStruct((4, local_rows, PICKS), jnp.bfloat16),
            jax.ShapeDtypeStruct((local_rows, NB), jnp.float32),
        ),
        in_specs=[SMEM] * 2 + [VMEM] * 5,
        out_specs=(HBM, HBM),
        scratch_shapes=[
            pltpu.VMEM((2, local_rows, NB), jnp.float32),
            pltpu.VMEM((4, local_rows, PICKS), jnp.bfloat16),
            pltpu.VMEM((local_rows, NB), jnp.float32),
            pltpu.SemaphoreType.DMA((2,)),
        ],
        compiler_params=pltpu.CompilerParams(vmem_limit_bytes=24 << 20),
        cost_estimate=pl.CostEstimate(flops=1_200_000_000, transcendentals=0, bytes_accessed=20_000_000),
        name="weigh",
    )(place, moved, panel, head, orders.reshape(3, PICKS), upper_inverse, lower_inverse)


def update_kernel(*refs):
    place, moved, weights_hbm, edge_hbm, rows_hbm = refs[:5]
    pieces, out_hbm = (refs[5:10], refs[10:15]), refs[15]
    rows, plane, result, weights, edge = refs[16:21]
    row_sems, piece_sems, out_sems, weight_sems = refs[21:]
    groups, half = rows.shape[0], plane.shape[3]
    is_home = place[0] < 2
    found = moved[4 * PICKS]
    begins = (0, 4, 8, 12, 14, 16)

    def fetch_rows(group):
        columns = pl.ds(group * GROUP, GROUP)
        return pltpu.make_async_copy(rows_hbm.at[:, columns, :], rows.at[group], row_sems.at[group])

    def fetch_piece(side, n, kind):
        count = begins[n + 1] - begins[n]
        part = pl.ds(kind * SHARE, SHARE)
        return pltpu.make_async_copy(
            pieces[side][n].at[:, part],
            plane.at[side, pl.ds(begins[n], count), part],
            piece_sems.at[side, n, kind],
        )

    def write(group, slot):
        return pltpu.make_async_copy(
            result.at[slot], out_hbm.at[:, pl.ds(group * GROUP, GROUP), :], out_sems.at[slot]
        )

    factors = [
        pltpu.make_async_copy(weights_hbm, weights, weight_sems.at[0]),
        pltpu.make_async_copy(edge_hbm, edge, weight_sems.at[1]),
    ]
    for factor in factors:
        factor.start()
    def start_pieces(side, kind):
        for n in range(5):
            fetch_piece(side, n, kind).start()

    start_pieces(0, 0)
    fetch_rows(0).start()
    start_pieces(0, 1)
    fetch_rows(1).start()

    for group in range(groups):
        slot, side = group % 2, group * GROUP // half
        begin = group * GROUP % half
        if begin == 0:
            for n in range(5):
                fetch_piece(side, n, 0).wait()
        if group == 0:
            for factor in factors:
                factor.wait()
            start_pieces(1, 0)
            start_pieces(1, 1)
        if group + 2 < groups:
            fetch_rows(group + 2).start()
        if group >= 2:
            write(group - 2, slot).wait()
        picked = plane[side, :, :SHARE, begin : begin + GROUP, :].reshape(PICKS, GROUP, NB)
        picked = pltpu.einshape("rcl->crl", picked)
        products = []
        for pair in range(GROUP // 2):
            right_high, right_low = halves(jnp.concatenate([picked[2 * pair], picked[2 * pair + 1]], axis=1))
            product = single(weights[2 * side], right_high)
            product += single(weights[2 * side], right_low)
            product += single(weights[2 * side + 1], right_high)
            products += [product[:, :NB], product[:, NB:]]
        product = pltpu.einshape("crl->rcl", jnp.stack(products, axis=0))
        if begin == 0:
            for n in range(5):
                fetch_piece(side, n, 1).wait()
        fetch_rows(group).wait()

        def patch(i, carry):
            at = moved[(1 + side) * PICKS + i]
            rows[group, moved[i], :, :] = plane[side, at // SHARE, SHARE + at % SHARE, begin : begin + GROUP, :]
            return carry

        lax.fori_loop(0, found, patch, 0)
        result[slot, :NB] = jnp.where(is_home, 0.0, rows[group, :NB]) - product[:NB]
        result[slot, NB:] = rows[group, NB:] - product[NB:]
        if group == 0:
            result[slot, :, 0, :] = edge[...]
        write(group, slot).start()
    for group in range(max(0, groups - 2), groups):
        write(group, group % 2).wait()


def update(place, moved, weights, edge, rows, pieces):
    local_rows, blocks, _ = rows.shape
    groups = blocks // GROUP
    pieces = [piece.reshape((-1, 2 * SHARE) + piece.shape[1:]) for side in pieces for piece in side]
    return pl.pallas_call(
        update_kernel,
        out_shape=jax.ShapeDtypeStruct(rows.shape, rows.dtype),
        in_specs=[SMEM] * 2 + [HBM] * 13,
        out_specs=HBM,
        scratch_shapes=[
            pltpu.VMEM((groups, local_rows, GROUP, NB), jnp.float32),
            pltpu.VMEM((2, PLANE, 2 * SHARE, blocks // 2, NB), jnp.float32),
            pltpu.VMEM((2, local_rows, GROUP, NB), jnp.float32),
            pltpu.VMEM((4, local_rows, PICKS), jnp.bfloat16),
            pltpu.VMEM((local_rows, NB), jnp.float32),
            pltpu.SemaphoreType.DMA((groups,)),
            pltpu.SemaphoreType.DMA((2, 5, 2)),
            pltpu.SemaphoreType.DMA((2,)),
            pltpu.SemaphoreType.DMA((2,)),
        ],
        compiler_params=pltpu.CompilerParams(vmem_limit_bytes=48 << 20),
        cost_estimate=pl.CostEstimate(flops=3_300_000_000, transcendentals=0, bytes_accessed=26_000_000),
        name="update",
    )(place, moved, weights, edge, rows, *pieces)


def local(matrix, pivots, upper_inverse, lower_inverse):
    me = lax.axis_index("prow")
    rows = matrix.reshape(matrix.shape[0] * NB, matrix.shape[3], NB)
    place = jnp.stack([me, lax.axis_index("pcol")]).astype(jnp.int32)
    pivots = pivots.reshape(-1)
    panel = lax.all_gather(rows[:, 0, :], "pcol", axis=0)
    held = leave_home(rows[:NB], me)
    picked, kept = exchange(pivots, rows.shape[0] * SIDE * PLANE)
    rank, most = ranks_of(picked)
    sent, pick_row, hub_source = deal(place, picked, rank, rows)
    received = swap_all(sent)
    copies, panel = climb(held, me, panel)
    moved, orders = tables(place, pivots, kept, rank)
    spare = lax.cond(
        most <= SHARE,
        lambda: jnp.zeros((SHARE,) + rows.shape[1:], rows.dtype),
        lambda: crowded(place, pick_row, hub_source, rows),
    )
    index = jnp.where(most <= SHARE, hub_source, -1)
    index, orders = lax.optimization_barrier((index, orders))
    left, right, head = pack(place, index, received, spare, copies)
    planes = [list(range(z * PLANE, (z + 1) * PLANE)) for z in range(SIDE)]
    head = lax.all_to_all(head, "prow", 0, 0, tiled=True, axis_index_groups=planes)
    lines = gather_line(left, "x"), gather_line(right, "y")
    last = neighbours(lines[1], "x")
    last, head = lax.optimization_barrier((last, head))
    hops = neighbours(lines[0], "y"), last
    head = lax.all_gather(head, "pcol", axis=0)
    pieces = [gather_across(*parts) for parts in zip(lines, hops, "yx")]
    weights, edge = weigh(place, moved, panel, head, orders, upper_inverse, lower_inverse)
    out = update(place, moved, weights, edge, rows, pieces)
    return out.reshape(matrix.shape)


def solution(mesh):
    return jax.shard_map(
        local,
        mesh=mesh,
        in_specs=(P(None, "prow", None, None, "pcol", None), P(), P(), P()),
        out_specs=P(None, "prow", None, None, "pcol", None),
        check_vma=False,
    )
```
